32 devices in a mesh: dp: 2 (over x), pipe: 4 (over z), mp: 4 (over y, core).
Axes of the slice: x: 2, y: 2, z: 4, core: 2. Of those that a mesh axis runs over, the one named last changes fastest.
Arguments:
- inputs: bfloat16 [4, 128, 1024], P(None, 'dp', 'mp'), may hold values from -6 to 6
- cotangent: bfloat16 [4, 128, 1024], P(None, 'dp', 'mp'), may hold values from -6 to 6
- gain: float32 [4, 1024], P('pipe'), may hold values from 0.25 to 1.75
- weight_in: bfloat16 [4, 1024, 32768], P('pipe', None, 'mp'), may hold values from -0.1875 to 0.1875
- weight_out: bfloat16 [4, 32768, 1024], P('pipe', 'mp'), may hold values from -0.03125 to 0.03125
Outputs:
- grad_in: bfloat16 [4, 1024, 32768], P('pipe', 'dp', 'mp')
- grad_out: bfloat16 [4, 32768, 1024], P('pipe', 'mp', 'dp')
- grad_gain: float32 [4, 1024], P('pipe', 'mp')
The draws below stay inside these ranges and needn't reach their ends.
All inputs are finite; a program needn't handle non-finite values.
Results may differ from the reference program's by a relative error of at most 0.023.
Values may be sent and summed in bfloat16 or wider, within the bound.
A program may use at most 128 MiB of HBM per device.

```python
import math
import jax
import jax.numpy as jnp
from jax import lax

D = 1024
FF = 32768
MICRO = 4
SEGMENTS = 4
MB_TOK = 128


def shard_levels(rng, shape, split, low, largest):
    def one(dim, shards_of):
        steps = jax.random.uniform(jax.random.fold_in(jax.random.fold_in(rng, 6), dim), (shards_of,), jnp.float32, low / len(split), largest / len(split))
        return jnp.repeat(jnp.exp(steps), shape[dim] // shards_of).reshape((-1,) + (1,) * (len(shape) - dim - 1))

    level = one(*split[0])
    for cut in split[1:]:
        level = level * one(*cut)
    return level


def gaussian(stream_key, extent, scale, most, pieces=(), kind=jnp.bfloat16):
    entries = jax.random.normal(stream_key, extent, jnp.float32) * scale
    if len(pieces) > 0:
        entries = shard_levels(stream_key, extent, pieces, -0.22, 0.18) * entries
    return jnp.clip(entries, min=-most, max=most).astype(kind)


def setup_inputs(seed: int = 0) -> dict:
    streams_of = jax.random.split(jax.random.key(seed), 6)
    inputs = gaussian(streams_of[0], (MICRO, MB_TOK, D), 1.0, 6.0, ((1, 2), (2, 4)))
    cotangent = gaussian(streams_of[1], (MICRO, MB_TOK, D), 1.0, 6.0, ((1, 2), (2, 4)))
    gain = jnp.clip(1.0 + 0.15 * jax.random.normal(streams_of[2], (SEGMENTS, D), jnp.float32), 0.25, 1.75)
    weight_in = gaussian(streams_of[3], (SEGMENTS, D, FF), D ** -0.5, 0.1875, ((0, 4), (2, 4)))
    weight_out = gaussian(streams_of[4], (SEGMENTS, FF, D), FF ** -0.5, 0.03125, ((0, 4), (1, 4)))
    return dict(inputs=inputs, cotangent=cotangent, gain=gain, weight_in=weight_in, weight_out=weight_out)


GELU_COEF = math.sqrt(2.0 / math.pi)
CUBIC_COEF = 0.044715
NORM_EPS = 1e-06

def gelu_parts(values):
    tangent = jnp.tanh(GELU_COEF * (values + CUBIC_COEF * values * values * values))
    output = 0.5 * values * (1.0 + tangent)
    derivative = 0.5 * (1.0 + tangent) + 0.5 * values * (1.0 - tangent * tangent) * GELU_COEF * (1.0 + 3.0 * CUBIC_COEF * values * values)
    return (output, derivative)

def reference(inputs, cotangent, gain, weight_in, weight_out):
    hidden_rows = inputs.reshape(-1, D)
    saved = []
    for segment in range(SEGMENTS):
        values = hidden_rows.astype(jnp.float32)
        inv_rms = lax.rsqrt(lax.optimization_barrier(jnp.mean(values * values, axis=1, keepdims=True)) + NORM_EPS)
        normed = (values * inv_rms * gain[segment]).astype(jnp.bfloat16)
        gate_input = jnp.dot(normed, weight_in[segment], preferred_element_type=jnp.float32)
        activated = gelu_parts(gate_input)[0].astype(jnp.bfloat16)
        branch = jnp.dot(activated, weight_out[segment], preferred_element_type=jnp.float32)
        saved.append((values, inv_rms, normed))
        hidden_rows = (values + branch).astype(jnp.bfloat16)
    grad_rows = cotangent.reshape(-1, D).astype(jnp.float32)
    grads_in = [None] * SEGMENTS
    grads_out = [None] * SEGMENTS
    grads_gain = [None] * SEGMENTS
    for segment in reversed(range(SEGMENTS)):
        values, inv_rms, normed = saved[segment]
        gate_input = jnp.dot(normed, weight_in[segment], preferred_element_type=jnp.float32)
        output_vals, slopes = gelu_parts(gate_input)
        activated = output_vals.astype(jnp.bfloat16)
        out_grad = grad_rows.astype(jnp.bfloat16)
        inner_grad = jnp.dot(out_grad, weight_out[segment].T, preferred_element_type=jnp.float32)
        pre_grad = (inner_grad * slopes).astype(jnp.bfloat16)
        grads_in[segment] = jnp.dot(normed.T, pre_grad, preferred_element_type=jnp.float32).astype(jnp.bfloat16)
        grads_out[segment] = jnp.dot(activated.T, out_grad, preferred_element_type=jnp.float32).astype(jnp.bfloat16)
        norm_grad = jnp.dot(pre_grad, weight_in[segment].T, preferred_element_type=jnp.float32)
        unit_rows = values * inv_rms
        grads_gain[segment] = lax.optimization_barrier(jnp.sum(norm_grad * unit_rows, axis=0))
        scaled = norm_grad * gain[segment]
        row_dot = lax.optimization_barrier(jnp.sum(scaled * unit_rows, axis=1, keepdims=True))
        grad_rows = grad_rows + inv_rms * (scaled - unit_rows * row_dot / D)
    return (jnp.stack(grads_in), jnp.stack(grads_out), jnp.stack(grads_gain))
```

```python
import functools
import math

import jax
import jax.numpy as jnp
from jax import lax
from jax.experimental import pallas as pl
from jax.experimental.pallas import tpu as pltpu
from jax.sharding import PartitionSpec as P

GELU_COEF = math.sqrt(2.0 / math.pi)
CUBIC_COEF = 0.044715
NORM_EPS = 1e-06
CONTRACT_LAST = (((1,), (1,)), ((), ()))
CONTRACT_FIRST = (((0,), (0,)), ((), ()))
MESH = pl.DeviceIdType.MESH


def gelu_parts(values):
    square = values * values
    half = 0.5 + 0.5 * jnp.tanh(values * (GELU_COEF + GELU_COEF * CUBIC_COEF * square))
    bend = values * (half - half * half)
    derivative = half + bend * (2.0 * GELU_COEF + 6.0 * GELU_COEF * CUBIC_COEF * square)
    return (values * half, derivative)


def inverse_rms(values):
    return lax.rsqrt(jnp.mean(values * values, axis=1, keepdims=True) + NORM_EPS)


def relay(
    sizes,
    x_ref,
    cot_ref,
    gain_ref,
    w1_hbm,
    w2_hbm,
    zt_out,
    p_out,
    ut_out,
    e_out,
    gain_out,
    w1,
    w2,
    z_keep,
    a_keep,
    p_keep,
    flip,
    h_all,
    u_all,
    ut,
    e_all,
    f_send,
    f_recv,
    b_send,
    b_recv,
    h_hop,
    g_hop,
    scale_all,
    dot_part,
    dot_recv,
    gain_part,
    gain_recv,
    w1_sem,
    w2_sem,
    zt_sem,
    p_sem,
    out_sem,
    x_ssem,
    x_rsem,
    hop_ssem,
    hop_rsem,
    mate_ssem,
    mate_rsem,
    side_ssem,
    side_rsem,
    pass_ssem,
    pass_rsem,
    u_ssem,
    u_rsem,
    rs_ssem,
    rs_rsem,
    dot_ssem,
    dot_rsem,
    gain_ssem,
    gain_rsem,
):
    stages, parts, replicas, hop_width = sizes
    sec = lax.axis_index("pipe")
    me = lax.axis_index("mp")
    rep = lax.axis_index("dp")
    tiles, full, tile = w1.shape
    rows = h_all.shape[0]
    own = rows // parts
    width = full // parts
    chunks = full // hop_width
    lag = 2
    first = sec == 0
    last = sec == stages - 1
    chips = parts // 2
    chip, core = me // 2, lax.rem(me, 2)
    mate = chip * 2 + 1 - core

    def w_copies(i):
        start = pl.multiple_of(i * tile, tile)
        return (
            pltpu.make_async_copy(w1_hbm.at[:, pl.ds(start, tile)], w1.at[i], w1_sem.at[i]),
            pltpu.make_async_copy(w2_hbm.at[pl.ds(start, tile), :], w2.at[i], w2_sem.at[i]),
        )

    for which in range(2):
        for i in range(tiles):
            w_copies(i)[which].start()

    def across_core(k):
        return lax.rem(chip + k, chips) * 2 + 1 - core

    barrier = pltpu.get_barrier_semaphore()
    peers = []
    for d in range(replicas):
        for j in range(parts):
            if d or j:
                peers.append((d, j, lax.rem(rep + d, replicas), lax.rem(me + j, parts)))
    for _, _, other, part in peers:
        pl.semaphore_signal(
            barrier, inc=1, device_id={"dp": other, "mp": part}, device_id_type=MESH
        )
    for step in (1, stages - 1):
        for k in range(chips):
            pl.semaphore_signal(
                barrier,
                inc=1,
                device_id={"pipe": lax.rem(sec + step, stages), "mp": across_core(k)},
                device_id_type=MESH,
            )
    dot_part[...] = jnp.zeros_like(dot_part)
    pl.semaphore_wait(barrier, len(peers) + 2 * chips)

    my_rows = pl.ds(pl.multiple_of(me * own, own), own)
    my_cols = pl.ds(pl.multiple_of(me * width, width), width)

    half = full // replicas
    kept = pl.ds(pl.multiple_of(rep * half, half), half)

    def remote(src, dst, ssem, rsem, where):
        return pltpu.make_async_remote_copy(
            src_ref=src,
            dst_ref=dst,
            send_sem=ssem,
            recv_sem=rsem,
            device_id=where,
            device_id_type=MESH,
        )

    def others():
        return [(j, lax.rem(me + j, parts)) for j in range(1, parts)]

    def columns(q):
        return pl.ds(pl.multiple_of(q * hop_width, hop_width), hop_width)

    def start(copies):
        for copy in copies:
            copy.start()

    def finish(copies):
        for copy in copies:
            copy.wait()

    def block_rows(k):
        block = lax.rem(chip + chips - k, chips) * 2 + 1 - core
        return pl.ds(pl.multiple_of(block * own, own), own)

    def hop_copies(src, dst, which, q, step):
        return [
            remote(
                src.at[:, columns(q)],
                dst.at[my_rows, columns(q)],
                hop_ssem.at[which, q, k],
                hop_rsem.at[which, q, k],
                {"pipe": lax.rem(sec + step, stages), "mp": across_core(k)},
            )
            for k in range(chips)
        ]

    def forward_hop(q):
        return hop_copies(h_hop, h_all, 0, q, 1)

    def backward_hop(q):
        return hop_copies(g_hop, e_all.at[0], 1, q, stages - 1)

    def mate_copies(ref, which, q):
        copies = []
        for k in range(chips):
            part = ref.at[block_rows(k), columns(q)]
            copies.append(
                remote(
                    part, part, mate_ssem.at[which, q, k], mate_rsem.at[which, q, k], {"mp": mate}
                )
            )
        return copies

    def side_copies(d, q):
        return [
            remote(
                e_all.at[0, block_rows(k), columns(q)],
                e_all.at[d, block_rows(k), columns(q)],
                side_ssem.at[d, q, k],
                side_rsem.at[d, q, k],
                {"dp": lax.rem(rep + d, replicas)},
            )
            for k in range(chips)
        ]

    def pass_copies(d, q):
        copies = []
        for k in range(chips):
            part = e_all.at[d, block_rows(k), columns(q)]
            copies.append(
                remote(part, part, pass_ssem.at[d, q, k], pass_rsem.at[d, q, k], {"mp": mate})
            )
        return copies

    def u_copies(d):
        part = pl.ds(pl.multiple_of(core * (rows // 2), rows // 2), rows // 2)
        there = {"dp": lax.rem(rep + d, replicas)}
        return (
            remote(u_all.at[0, part], u_all.at[d, part], u_ssem.at[0, d], u_rsem.at[0, d], there),
            remote(
                u_all.at[d, part], u_all.at[d, part], u_ssem.at[1, d], u_rsem.at[1, d], {"mp": mate}
            ),
        )

    def gather_features(src, dst):
        def cols(k):
            block = lax.rem(chip + chips - k, chips) * 2 + core
            return pl.ds(pl.multiple_of(block * width, width), width)

        def across(k):
            target = lax.rem(chip + k, chips) * 2 + core
            return remote(src, dst.at[:, my_cols], x_ssem.at[k], x_rsem.at[k], {"mp": target})

        def beside(k):
            part = dst.at[:, cols(k)]
            slot = chips + k
            return remote(
                src if k == 0 else part, part, x_ssem.at[slot], x_rsem.at[slot], {"mp": mate}
            )

        for k in range(1, chips):
            across(k).start()
        beside(0).start()
        dst[:, my_cols] = src[...]
        for k in range(1, chips):
            across(k).wait_recv()
            beside(k).start()
        for k in range(1, chips):
            across(k).wait_send()
        for k in range(chips):
            beside(k).wait()

    def sum_copies(src, dst, which, q):
        return [
            remote(
                src.at[pl.ds(pl.multiple_of(part * own, own), own), columns(q)],
                dst.at[j, :, columns(q)],
                rs_ssem.at[which, q, j],
                rs_rsem.at[which, q, j],
                {"mp": part},
            )
            for j, part in others()
        ]

    def dot_copies():
        return [
            remote(
                dot_part.at[pl.ds(pl.multiple_of(part * own, own), own)],
                dot_recv.at[j],
                dot_ssem.at[j],
                dot_rsem.at[j],
                {"mp": part},
            )
            for j, part in others()
        ]

    step_width = math.gcd(tile, 256)
    steps = tile // step_width
    lanes = scale_all.shape[1]

    def staged(product, use):
        held = product(0)
        for s in range(1, steps):
            ahead = product(s)
            use(s - 1, held)
            held = ahead
        use(steps - 1, held)

    def fold(values):
        total = values[:, :lanes]
        for c in range(lanes, values.shape[1], lanes):
            total += values[:, c : c + lanes]
        return total

    def spread(values, count):
        return jnp.concatenate([values] * (count // lanes), axis=1)

    def activate(d, i, kind):
        def product(s):
            piece = w1[i, :, s * step_width : (s + 1) * step_width]
            return jnp.dot(u_all[d], piece, preferred_element_type=jnp.float32)

        def use(s, gate):
            place = slice(s * step_width, (s + 1) * step_width)
            if kind != "other":
                gate = gate * spread(scale_all[...], step_width)
            output, slope = gelu_parts(gate)
            z_keep[i, :, place] = output.astype(jnp.bfloat16)
            if kind == "own":
                a_keep[i, :, place] = gate.astype(jnp.bfloat16)
            if kind == "last":
                slope = slope * p_keep[d, i, :, place].astype(jnp.float32)
                dot_part[...] += fold(slope * gate)
            p_keep[d, i, :, place] = slope.astype(jnp.bfloat16)

        staged(product, use)

    def pregrad(d, i, kind):
        def product(s):
            piece = w2[i, s * step_width : (s + 1) * step_width, :]
            return lax.dot_general(
                e_all[d], piece, CONTRACT_LAST, preferred_element_type=jnp.float32
            )

        def use(s, inner):
            place = slice(s * step_width, (s + 1) * step_width)
            if kind != "plain":
                inner = inner * p_keep[d, i, :, place].astype(jnp.float32)
            if kind == "own":
                dot_part[...] += fold(inner * a_keep[i, :, place].astype(jnp.float32))
            p_keep[d, i, :, place] = inner.astype(jnp.bfloat16)

        staged(product, use)

    def p_copy(d, i):
        return pltpu.make_async_copy(
            p_keep.at[d, i],
            p_out.at[pl.ds(d * rows, rows), pl.ds(pl.multiple_of(i * tile, tile), tile)],
            p_sem.at[d, i],
        )

    def zt_copy(d, i, slot):
        return pltpu.make_async_copy(
            flip.at[slot],
            zt_out.at[pl.ds(pl.multiple_of(i * tile, tile), tile), pl.ds(d * rows, rows)],
            zt_sem.at[slot],
        )

    def turn(d, i):
        slot = lax.rem(i, 2)

        @pl.when(i >= 2)
        def _():
            zt_copy(d, i - 2, slot).wait()

        for s in range(steps):
            place = slice(s * step_width, (s + 1) * step_width)
            flip[slot, place, :] = z_keep[i, :, place].astype(jnp.float32).T.astype(jnp.bfloat16)
        zt_copy(d, i, slot).start()

    def turned(d):
        for i in range(max(0, tiles - 2), tiles):
            zt_copy(d, i, i % 2).wait()

    def side_start():
        for q in range(chunks):
            for d in range(1, replicas):
                start(side_copies(d, q))

    @pl.when(last)
    def _():
        gather_features(cot_ref, e_all.at[0])
        side_start()

        @pl.loop(0, tiles)
        def _(i):
            w_copies(i)[1].wait()
            pregrad(0, i, "plain")

    def prepare(cols):
        values = h_all[:, cols].astype(jnp.float32)
        u_all[0, :, cols] = (values * gain_ref[:, cols]).astype(jnp.bfloat16)
        return fold(values * values)

    def close(squares):
        scale = lax.rsqrt(jnp.sum(squares, axis=1, keepdims=True) / full + NORM_EPS)
        scale_all[...] = jnp.broadcast_to(scale, scale_all.shape)

    @pl.when(first)
    def _():
        gather_features(x_ref, h_all)
        squares = prepare(slice(0, hop_width))
        for q in range(1, chunks):
            squares += prepare(slice(q * hop_width, (q + 1) * hop_width))
        close(squares)

    @pl.when(jnp.logical_not(first))
    def _():
        for copy in forward_hop(0):
            copy.wait_recv()
        start(mate_copies(h_all, 0, 0))
        squares = jnp.zeros((rows, lanes), jnp.float32)
        for q in range(chunks):
            if q + 1 < chunks:
                for copy in forward_hop(q + 1):
                    copy.wait_recv()
                start(mate_copies(h_all, 0, q + 1))
            finish(mate_copies(h_all, 0, q))
            squares += prepare(slice(q * hop_width, (q + 1) * hop_width))
        close(squares)

    def normed():
        values = h_all[...].astype(jnp.float32)
        u_all[0] = (values * scale_all[:, 0:1] * gain_ref[...]).astype(jnp.bfloat16)
        for d in range(1, replicas):
            u_copies(d)[0].start()

    @pl.when(last)
    def _():
        @pl.loop(0, tiles)
        def _(i):
            w_copies(i)[0].wait()
            activate(0, i, "last")
            p_copy(0, i).start()

        start(dot_copies())

    def pass_on(q):
        total = h_all[my_rows, columns(q)].astype(jnp.float32)
        total += f_send[my_rows, columns(q)].astype(jnp.float32)
        for j, copy in enumerate(sum_copies(f_send, f_recv, 0, q)):
            copy.wait()
            total += f_recv[j + 1, :, columns(q)].astype(jnp.float32)
        h_hop[:, columns(q)] = total.astype(jnp.bfloat16)
        start(forward_hop(q))

    @pl.when(jnp.logical_not(last))
    def _():
        @pl.loop(0, tiles)
        def _(i):
            w_copies(i)[0].wait()
            activate(0, i, "own")

        @pl.loop(0, tiles)
        def _(i):
            w_copies(i)[1].wait()

        @pl.loop(0, chunks)
        def _(q):
            total = jnp.zeros((rows, hop_width), jnp.float32)
            for i in range(tiles):
                total += jnp.dot(
                    z_keep[i], w2[i, :, columns(q)], preferred_element_type=jnp.float32
                )
            f_send[:, columns(q)] = total.astype(jnp.bfloat16)
            start(sum_copies(f_send, f_recv, 0, q))

            @pl.when(q >= lag)
            def _():
                pass_on(q - lag)

        for q in range(max(0, chunks - lag), chunks):
            pass_on(q)

    def replica_forward():
        normed()

        @pl.loop(0, tiles)
        def _(i):
            turn(0, i)

        turned(0)
        for d in range(1, replicas):
            u_copies(d)[0].wait_recv()
            u_copies(d)[1].start()
        for d in range(1, replicas):
            u_copies(d)[1].wait()
            u_copies(d)[0].wait_send()

            @pl.loop(0, tiles)
            def _(i):
                activate(d, i, "other")
                turn(d, i)

            turned(d)

        for d in range(replicas):
            flipped = u_all[d, :, kept].astype(jnp.float32).T
            ut[:, d * rows : (d + 1) * rows] = flipped.astype(jnp.bfloat16)
        pltpu.make_async_copy(ut, ut_out, out_sem.at[0, 0]).start()

    @pl.when(jnp.logical_not(last))
    def _():
        replica_forward()
        for q in range(chunks):
            for copy in forward_hop(q):
                copy.wait_send()
        for q in range(chunks):
            for copy in backward_hop(q):
                copy.wait_recv()
            start(mate_copies(e_all.at[0], 1, q))
            for d in range(1, replicas):
                start(side_copies(d, q))
        for q in range(chunks):
            finish(mate_copies(e_all.at[0], 1, q))

        @pl.loop(0, tiles)
        def _(i):
            pregrad(0, i, "own")
            p_copy(0, i).start()

        @pl.when(jnp.logical_not(first))
        def _():
            start(dot_copies())

    for q in range(chunks):
        for d in range(1, replicas):
            for copy in side_copies(d, q):
                copy.wait_recv()
            start(pass_copies(d, q))

    def pass_back(q, shift):
        total = b_send[my_rows, columns(q)].astype(jnp.float32)
        for j, copy in enumerate(sum_copies(b_send, b_recv, 1, q)):
            copy.wait()
            total += b_recv[j + 1, :, columns(q)].astype(jnp.float32)
        scale = scale_all[my_rows, 0:1]
        unit = h_all[my_rows, columns(q)].astype(jnp.float32) * scale
        previous = e_all[0, my_rows, columns(q)].astype(jnp.float32) + scale * (
            total * gain_ref[:, columns(q)] - unit * shift
        )
        g_hop[:, columns(q)] = previous.astype(jnp.bfloat16)
        start(backward_hop(q))

    def row_shift():
        total = dot_part[my_rows, :]
        for j in range(1, parts):
            total += dot_recv[j]
        return jnp.sum(total, axis=1, keepdims=True) / full

    @pl.loop(0, chunks)
    def _(q):
        total = jnp.zeros((rows, hop_width), jnp.float32)
        for i in range(tiles):
            total += lax.dot_general(
                p_keep[0, i], w1[i, columns(q), :], CONTRACT_LAST, preferred_element_type=jnp.float32
            )

        @pl.when(jnp.logical_not(first))
        def _():
            b_send[:, columns(q)] = total.astype(jnp.bfloat16)
            start(sum_copies(b_send, b_recv, 1, q))

        unit = h_all[:, columns(q)].astype(jnp.float32) * spread(scale_all[...], hop_width)
        gain_part[:, columns(q)] = jnp.sum(
            (total * unit).reshape(rows // 8, 8, hop_width), axis=0
        )

        @pl.when(jnp.logical_not(first))
        def _():
            @pl.when(q == lag)
            def _():
                finish(dot_copies())

            @pl.when(q >= lag)
            def _():
                pass_back(q - lag, row_shift())

    @pl.when(jnp.logical_not(first))
    def _():
        for q in range(max(0, chunks - lag), chunks):
            pass_back(q, row_shift())

    gain_copies = [
        remote(
            gain_part.at[:, pl.ds(pl.multiple_of(part * width, width), width)],
            gain_recv.at[d * parts + j],
            gain_ssem.at[d * parts + j],
            gain_rsem.at[d * parts + j],
            {"dp": other, "mp": part},
        )
        for d, j, other, part in peers
    ]
    start(gain_copies)

    @pl.when(last)
    def _():
        replica_forward()

    for q in range(chunks):
        for d in range(1, replicas):
            finish(pass_copies(d, q))
            for copy in side_copies(d, q):
                copy.wait_send()
    for d in range(1, replicas):

        @pl.loop(0, tiles)
        def _(i):
            pregrad(d, i, "other")
            p_copy(d, i).start()

    outs = []
    for d in range(replicas):
        place = pl.ds(d * rows, rows)
        outs.append(pltpu.make_async_copy(e_all.at[d, :, kept], e_out.at[place, :], out_sem.at[1, d]))
    start(outs)
    outs.append(pltpu.make_async_copy(ut, ut_out, out_sem.at[0, 0]))
    total = gain_part[:, my_cols]
    for (d, j, _, _), copy in zip(peers, gain_copies):
        copy.wait()
        total += gain_recv[d * parts + j]
    gain_out[...] = jnp.sum(total, axis=0, keepdims=True)

    for d in range(replicas):

        @pl.loop(0, tiles)
        def _(i):
            p_copy(d, i).wait()

    finish(outs)

    @pl.when(jnp.logical_not(first))
    def _():
        for q in range(chunks):
            for copy in backward_hop(q):
                copy.wait_send()


def weight_grads(u_ref, e_ref, gain_ref, p_ref, zt_ref, in_ref, out_ref, gain_out):
    in_ref[...] = jnp.dot(
        u_ref[...], p_ref[...], preferred_element_type=jnp.float32
    ).astype(in_ref.dtype)
    out_ref[...] = jnp.dot(
        zt_ref[...], e_ref[...], preferred_element_type=jnp.float32
    ).astype(out_ref.dtype)
    gain_out[...] = gain_ref[...]


def shards(inputs, cotangent, gain, weight_in, weight_out):
    stages = lax.axis_size("pipe")
    parts = lax.axis_size("mp")
    replicas = lax.axis_size("dp")
    micro, row_count, width = inputs.shape
    rows = micro * row_count
    full = gain.shape[1]
    hidden = weight_in.shape[2]
    tile = math.gcd(hidden, 1024)
    tiles = hidden // tile
    own = rows // parts
    chips = parts // 2
    half = full // replicas
    hop_width = math.gcd(full, 256)
    chunks = full // hop_width
    lanes = 128
    count = replicas * rows
    bf16, f32 = jnp.bfloat16, jnp.float32
    vmem = pl.BlockSpec(memory_space=pltpu.VMEM)
    anywhere = pl.BlockSpec(memory_space=pl.ANY)
    dma = pltpu.SemaphoreType.DMA
    zt_all, p_all, u_flip, e_cols, gain_total = pl.pallas_call(
        functools.partial(relay, (stages, parts, replicas, hop_width)),
        name="relay",
        out_shape=(
            jax.ShapeDtypeStruct((hidden, count), bf16),
            jax.ShapeDtypeStruct((count, hidden), bf16),
            jax.ShapeDtypeStruct((half, count), bf16),
            jax.ShapeDtypeStruct((count, half), bf16),
            jax.ShapeDtypeStruct((1, width), f32),
        ),
        in_specs=[vmem, vmem, vmem, anywhere, anywhere],
        out_specs=(anywhere, anywhere, anywhere, anywhere, vmem),
        scratch_shapes=[
            pltpu.VMEM((tiles, full, tile), bf16),
            pltpu.VMEM((tiles, tile, full), bf16),
            pltpu.VMEM((tiles, rows, tile), bf16),
            pltpu.VMEM((tiles, rows, tile), bf16),
            pltpu.VMEM((replicas, tiles, rows, tile), bf16),
            pltpu.VMEM((2, tile, rows), bf16),
            pltpu.VMEM((rows, full), bf16),
            pltpu.VMEM((replicas, rows, full), bf16),
            pltpu.VMEM((half, count), bf16),
            pltpu.VMEM((replicas, rows, full), bf16),
            pltpu.VMEM((rows, full), bf16),
            pltpu.VMEM((parts, own, full), bf16),
            pltpu.VMEM((rows, full), bf16),
            pltpu.VMEM((parts, own, full), bf16),
            pltpu.VMEM((own, full), bf16),
            pltpu.VMEM((own, full), bf16),
            pltpu.VMEM((rows, lanes), f32),
            pltpu.VMEM((rows, lanes), f32),
            pltpu.VMEM((parts, own, lanes), f32),
            pltpu.VMEM((8, full), f32),
            pltpu.VMEM((replicas * parts, 8, width), f32),
            dma((tiles,)),
            dma((tiles,)),
            dma((2,)),
            dma((replicas, tiles)),
            dma((2, replicas)),
            dma((parts,)),
            dma((parts,)),
            dma((2, chunks, chips)),
            dma((2, chunks, chips)),
            dma((2, chunks, chips)),
            dma((2, chunks, chips)),
            dma((replicas, chunks, chips)),
            dma((replicas, chunks, chips)),
            dma((replicas, chunks, chips)),
            dma((replicas, chunks, chips)),
            dma((2, replicas)),
            dma((2, replicas)),
            dma((2, chunks, parts)),
            dma((2, chunks, parts)),
            dma((parts,)),
            dma((parts,)),
            dma((replicas * parts,)),
            dma((replicas * parts,)),
        ],
        compiler_params=pltpu.CompilerParams(
            collective_id=0, has_side_effects=True, vmem_limit_bytes=67043328
        ),
    )(
        inputs.reshape(rows, width),
        cotangent.reshape(rows, width),
        gain,
        weight_in[0],
        weight_out[0],
    )
    grad_first, grad_second, gain_sum = pl.pallas_call(
        weight_grads,
        name="weight_grads",
        grid=(tiles,),
        out_shape=(
            jax.ShapeDtypeStruct((half, hidden), bf16),
            jax.ShapeDtypeStruct((hidden, half), bf16),
            jax.ShapeDtypeStruct((1, width), f32),
        ),
        in_specs=[
            vmem,
            vmem,
            vmem,
            pl.BlockSpec((count, tile), lambda i: (0, i)),
            pl.BlockSpec((tile, count), lambda i: (i, 0)),
        ],
        out_specs=(
            pl.BlockSpec((half, tile), lambda i: (0, i)),
            pl.BlockSpec((tile, half), lambda i: (i, 0)),
            pl.BlockSpec((1, width), lambda i: (0, 0)),
        ),
        compiler_params=pltpu.CompilerParams(vmem_limit_bytes=67043328),
    )(u_flip, e_cols, gain_total, p_all, zt_all)
    return (grad_first[None], grad_second[None], gain_sum)


def solution(mesh):
    in_specs = (
        P(None, "dp", "mp"),
        P(None, "dp", "mp"),
        P("pipe", None),
        P("pipe", None, "mp"),
        P("pipe", "mp", None),
    )
    out_specs = (P("pipe", "dp", "mp"), P("pipe", "mp", "dp"), P("pipe", "mp"))
    return jax.shard_map(shards, mesh=mesh, in_specs=in_specs, out_specs=out_specs, check_vma=False)
```

```python
import functools
import math

import jax
import jax.numpy as jnp
from jax import lax
from jax.experimental import pallas as pl
from jax.experimental.pallas import tpu as pltpu
from jax.sharding import PartitionSpec as P

GELU_COEF = math.sqrt(2.0 / math.pi)
CUBIC_COEF = 0.044715
NORM_EPS = 1e-06
CONTRACT_LAST = (((1,), (1,)), ((), ()))
MESH = pl.DeviceIdType.MESH


CUBE = CUBIC_COEF / (GELU_COEF * GELU_COEF)
HALF_BACK = 0.5 / GELU_COEF


def gelu_tanh(y):
    bent = y * (CUBE * (y * y))
    return (bent, jnp.tanh(y + bent))


def gelu_value(y, tangent):
    return y * (1.0 + tangent)


def gelu_slope(y, bent, tangent):
    return (1.0 + tangent) + (1.0 - tangent * tangent) * (y + 3.0 * bent)


def relay(
    sizes,
    x_ref,
    cot_ref,
    gain_ref,
    w1_hbm,
    w2_hbm,
    zt_all,
    p_all,
    ut,
    e_cols,
    gain_out,
    w1,
    w2,
    z_keep,
    a_keep,
    h_all,
    u_all,
    e_all,
    f_send,
    f_recv,
    b_send,
    b_recv,
    h_hop,
    g_hop,
    scale_all,
    bend_all,
    dot_part,
    dot_recv,
    gain_part,
    gain_recv,
    w1_sem,
    w2_sem,
    out_sem,
    x_ssem,
    x_rsem,
    hop_ssem,
    hop_rsem,
    mate_ssem,
    mate_rsem,
    side_ssem,
    side_rsem,
    pass_ssem,
    pass_rsem,
    u_ssem,
    u_rsem,
    rs_ssem,
    rs_rsem,
    dot_ssem,
    dot_rsem,
    gain_ssem,
    gain_rsem,
):
    stages, parts, replicas, hop_width, span = sizes
    sec = lax.axis_index("pipe")
    me = lax.axis_index("mp")
    rep = lax.axis_index("dp")
    tiles, full, tile = w1.shape
    rows = h_all.shape[0]
    own = rows // parts
    width = full // parts
    chunks = full // hop_width
    lag = 2
    first = sec == 0
    last = sec == stages - 1
    chips = parts // 2
    chip, core = me // 2, lax.rem(me, 2)
    mate = chip * 2 + 1 - core

    def w_copies(i):
        start = pl.multiple_of(i * tile, tile)
        return (
            pltpu.make_async_copy(w1_hbm.at[:, pl.ds(start, tile)], w1.at[i], w1_sem.at[i]),
            pltpu.make_async_copy(w2_hbm.at[pl.ds(start, tile), :], w2.at[i], w2_sem.at[i]),
        )

    for which in range(2):
        for i in range(tiles):
            w_copies(i)[which].start()

    def across_core(k):
        return lax.rem(chip + k, chips) * 2 + 1 - core

    barrier = pltpu.get_barrier_semaphore()
    peers = []
    for d in range(replicas):
        for j in range(parts):
            if d or j:
                peers.append((d, j, lax.rem(rep + d, replicas), lax.rem(me + j, parts)))
    for _, _, other, part in peers:
        pl.semaphore_signal(
            barrier, inc=1, device_id={"dp": other, "mp": part}, device_id_type=MESH
        )
    for step in (1, stages - 1):
        for k in range(chips):
            pl.semaphore_signal(
                barrier,
                inc=1,
                device_id={"pipe": lax.rem(sec + step, stages), "mp": across_core(k)},
                device_id_type=MESH,
            )
    dot_part[...] = jnp.zeros_like(dot_part)
    pl.semaphore_wait(barrier, len(peers) + 2 * chips)

    my_rows = pl.ds(pl.multiple_of(me * own, own), own)
    my_cols = pl.ds(pl.multiple_of(me * width, width), width)

    half = full // replicas
    kept = pl.ds(pl.multiple_of(rep * half, half), half)

    def remote(src, dst, ssem, rsem, where):
        return pltpu.make_async_remote_copy(
            src_ref=src,
            dst_ref=dst,
            send_sem=ssem,
            recv_sem=rsem,
            device_id=where,
            device_id_type=MESH,
        )

    def others():
        return [(j, lax.rem(me + j, parts)) for j in range(1, parts)]

    def columns(q):
        return pl.ds(pl.multiple_of(q * hop_width, hop_width), hop_width)

    blocks = chunks // span
    block_width = hop_width * span

    def block_columns(b):
        return pl.ds(pl.multiple_of(b * block_width, block_width), block_width)

    def start(copies):
        for copy in copies:
            copy.start()

    def finish(copies):
        for copy in copies:
            copy.wait()

    def block_rows(k):
        block = lax.rem(chip + chips - k, chips) * 2 + 1 - core
        return pl.ds(pl.multiple_of(block * own, own), own)

    def hop_copies(src, dst, which, q, step):
        return [
            remote(
                src.at[:, columns(q)],
                dst.at[my_rows, columns(q)],
                hop_ssem.at[which, q, k],
                hop_rsem.at[which, q, k],
                {"pipe": lax.rem(sec + step, stages), "mp": across_core(k)},
            )
            for k in range(chips)
        ]

    def forward_hop(q):
        return hop_copies(h_hop, h_all, 0, q, 1)

    def backward_hop(q):
        return hop_copies(g_hop, e_all.at[0], 1, q, stages - 1)

    def mate_copies(ref, which, q):
        copies = []
        for k in range(chips):
            part = ref.at[block_rows(k), columns(q)]
            copies.append(
                remote(
                    part, part, mate_ssem.at[which, q, k], mate_rsem.at[which, q, k], {"mp": mate}
                )
            )
        return copies

    def side_copies(d):
        return [
            remote(
                e_all.at[0, block_rows(k)],
                e_all.at[d, block_rows(k)],
                side_ssem.at[d, k],
                side_rsem.at[d, k],
                {"dp": lax.rem(rep + d, replicas)},
            )
            for k in range(chips)
        ]

    def pass_copies(d):
        copies = []
        for k in range(chips):
            part = e_all.at[d, block_rows(k)]
            copies.append(
                remote(part, part, pass_ssem.at[d, k], pass_rsem.at[d, k], {"mp": mate})
            )
        return copies

    def u_copies(d):
        part = pl.ds(pl.multiple_of(core * (rows // 2), rows // 2), rows // 2)
        there = {"dp": lax.rem(rep + d, replicas)}
        return (
            remote(u_all.at[0, part], u_all.at[d, part], u_ssem.at[0, d], u_rsem.at[0, d], there),
            remote(
                u_all.at[d, part], u_all.at[d, part], u_ssem.at[1, d], u_rsem.at[1, d], {"mp": mate}
            ),
        )

    def gather_features(src, dst):
        def cols(k):
            block = lax.rem(chip + chips - k, chips) * 2 + core
            return pl.ds(pl.multiple_of(block * width, width), width)

        def across(k):
            target = lax.rem(chip + k, chips) * 2 + core
            return remote(src, dst.at[:, my_cols], x_ssem.at[k], x_rsem.at[k], {"mp": target})

        def beside(k):
            part = dst.at[:, cols(k)]
            slot = chips + k
            return remote(
                src if k == 0 else part, part, x_ssem.at[slot], x_rsem.at[slot], {"mp": mate}
            )

        for k in range(1, chips):
            across(k).start()
        beside(0).start()
        dst[:, my_cols] = src[...]
        for k in range(1, chips):
            across(k).wait_recv()
            beside(k).start()
        for k in range(1, chips):
            across(k).wait_send()
        for k in range(chips):
            beside(k).wait()

    def sum_copies(src, dst, which, q):
        return [
            remote(
                src.at[pl.ds(pl.multiple_of(part * own, own), own), columns(q)],
                dst.at[j - 1, :, columns(q)],
                rs_ssem.at[which, q, j],
                rs_rsem.at[which, q, j],
                {"mp": part},
            )
            for j, part in others()
        ]

    def dot_copies():
        return [
            remote(
                dot_part.at[pl.ds(pl.multiple_of(part * own, own), own)],
                dot_recv.at[j - 1],
                dot_ssem.at[j],
                dot_rsem.at[j],
                {"mp": part},
            )
            for j, part in others()
        ]

    step_width = math.gcd(tile, 256)
    steps = tile // step_width
    lanes = scale_all.shape[1]

    def staged(product, use):
        held = product(0)
        for s in range(1, steps):
            ahead = product(s)
            use(s - 1, held)
            held = ahead
        use(steps - 1, held)

    def fold(values):
        total = values[:, :lanes]
        for c in range(lanes, values.shape[1], lanes):
            total += values[:, c : c + lanes]
        return total

    def spread(values, count):
        return jnp.concatenate([values] * (count // lanes), axis=1)

    def spot(d, i, s):
        return i, slice(d * rows, (d + 1) * rows), slice(s * step_width, (s + 1) * step_width)

    def activate(d, i, kind):
        def product(s):
            piece = w1[i, :, s * step_width : (s + 1) * step_width]
            return jnp.dot(u_all[d], piece, preferred_element_type=jnp.float32)

        def use(s, gate):
            place = slice(s * step_width, (s + 1) * step_width)
            if kind == "other":
                y = gate * GELU_COEF
            else:
                y = gate * spread(bend_all[...], step_width)
                a_keep[i, :, place] = y.astype(jnp.bfloat16)
            if kind == "own":
                y = y.astype(jnp.bfloat16)
            bent, tangent = gelu_tanh(y)
            if kind != "last":
                z_keep[i, :, place] = gelu_value(y, tangent).astype(jnp.bfloat16)
            if kind != "own":
                slope = gelu_slope(y, bent, tangent)
                if kind == "last":
                    slope = slope * p_all[spot(d, i, s)].astype(jnp.float32)
                    dot_part[...] += fold(slope * y)
                p_all[spot(d, i, s)] = slope.astype(jnp.bfloat16)

        staged(product, use)

    def complete(i, kind):
        for s in range(steps):
            place = slice(s * step_width, (s + 1) * step_width)
            y = a_keep[i, :, place].astype(jnp.float32)
            bent, tangent = gelu_tanh(y)
            if kind == "own":
                p_all[spot(0, i, s)] = gelu_slope(y, bent, tangent).astype(jnp.bfloat16)
            else:
                z_keep[i, :, place] = gelu_value(y, tangent).astype(jnp.bfloat16)

    def pregrad(d, i, kind):
        def product(s):
            piece = w2[i, s * step_width : (s + 1) * step_width, :]
            return lax.dot_general(
                e_all[d], piece, CONTRACT_LAST, preferred_element_type=jnp.float32
            )

        def use(s, inner):
            place = slice(s * step_width, (s + 1) * step_width)
            if kind != "plain":
                inner = inner * p_all[spot(d, i, s)].astype(jnp.float32)
            if kind == "own":
                dot_part[...] += fold(inner * a_keep[i, :, place].astype(jnp.float32))
            p_all[spot(d, i, s)] = inner.astype(jnp.bfloat16)

        staged(product, use)

    def turn(d, i):
        for s in range(steps):
            place = slice(s * step_width, (s + 1) * step_width)
            down = pl.ds(pl.multiple_of(i * tile + s * step_width, step_width), step_width)
            flipped = z_keep[i, :, place].astype(jnp.float32).T
            zt_all[down, d * rows : (d + 1) * rows] = flipped.astype(jnp.bfloat16)

    def side_start():
        for d in range(1, replicas):
            start(side_copies(d))

    @pl.when(last)
    def _():
        gather_features(cot_ref, e_all.at[0])
        side_start()

        @pl.loop(0, tiles)
        def _(i):
            w_copies(i)[1].wait()
            pregrad(0, i, "plain")

    def prepare(cols):
        values = h_all[:, cols].astype(jnp.float32)
        u_all[0, :, cols] = (values * gain_ref[:, cols]).astype(jnp.bfloat16)
        return fold(values * values)

    def close(squares):
        scale = lax.rsqrt(jnp.sum(squares, axis=1, keepdims=True) / full + NORM_EPS)
        scale_all[...] = jnp.broadcast_to(scale, scale_all.shape)
        bend_all[...] = scale_all[...] * GELU_COEF

    @pl.when(first)
    def _():
        gather_features(x_ref, h_all)
        squares = prepare(slice(0, hop_width))
        for q in range(1, chunks):
            squares += prepare(slice(q * hop_width, (q + 1) * hop_width))
        close(squares)

    @pl.when(jnp.logical_not(first))
    def _():
        for copy in forward_hop(0):
            copy.wait_recv()
        start(mate_copies(h_all, 0, 0))
        squares = jnp.zeros((rows, lanes), jnp.float32)
        for q in range(chunks):
            if q + 1 < chunks:
                for copy in forward_hop(q + 1):
                    copy.wait_recv()
                start(mate_copies(h_all, 0, q + 1))
            finish(mate_copies(h_all, 0, q))
            squares += prepare(slice(q * hop_width, (q + 1) * hop_width))
        close(squares)

    def normed():
        values = h_all[...].astype(jnp.float32)
        u_all[0] = (values * scale_all[:, 0:1] * gain_ref[...]).astype(jnp.bfloat16)
        for d in range(1, replicas):
            u_copies(d)[0].start()

    @pl.when(last)
    def _():
        @pl.loop(0, tiles)
        def _(i):
            w_copies(i)[0].wait()
            activate(0, i, "last")

        start(dot_copies())

    def pass_on(q):
        total = h_all[my_rows, columns(q)].astype(jnp.float32)
        total += f_send[my_rows, columns(q)].astype(jnp.float32)
        for j, copy in enumerate(sum_copies(f_send, f_recv, 0, q)):
            copy.wait()
            total += f_recv[j, :, columns(q)].astype(jnp.float32)
        h_hop[:, columns(q)] = total.astype(jnp.bfloat16)
        start(forward_hop(q))

    @pl.when(jnp.logical_not(last))
    def _():
        @pl.loop(0, tiles)
        def _(i):
            w_copies(i)[0].wait()
            activate(0, i, "own")

        @pl.loop(0, tiles)
        def _(i):
            w_copies(i)[1].wait()

        @pl.loop(0, blocks)
        def _(b):
            total = jnp.zeros((rows, block_width), jnp.float32)
            for i in range(tiles):
                total += jnp.dot(
                    z_keep[i], w2[i, :, block_columns(b)], preferred_element_type=jnp.float32
                )
            f_send[:, block_columns(b)] = (total * HALF_BACK).astype(jnp.bfloat16)
            for t in range(span):
                start(sum_copies(f_send, f_recv, 0, b * span + t))

            @pl.when(b >= lag)
            def _():
                for t in range(span):
                    pass_on((b - lag) * span + t)

        for q in range(max(0, blocks - lag) * span, chunks):
            pass_on(q)

    def replica_forward(kind):
        normed()

        @pl.loop(0, tiles)
        def _(i):
            complete(i, kind)
            turn(0, i)

        for d in range(1, replicas):
            u_copies(d)[0].wait_recv()
            u_copies(d)[1].start()
        flip_u(0)
        for d in range(1, replicas):
            u_copies(d)[1].wait()
            u_copies(d)[0].wait_send()

            @pl.loop(0, tiles)
            def _(i):
                activate(d, i, "other")
                turn(d, i)

            flip_u(d)

    def flip_u(d):
        flipped = u_all[d, :, kept].astype(jnp.float32).T
        ut[:, d * rows : (d + 1) * rows] = flipped.astype(jnp.bfloat16)

    @pl.when(jnp.logical_not(last))
    def _():
        replica_forward("own")
        for q in range(chunks):
            for copy in forward_hop(q):
                copy.wait_send()
        for q in range(chunks):
            for copy in backward_hop(q):
                copy.wait_recv()
            start(mate_copies(e_all.at[0], 1, q))
        for q in range(chunks):
            finish(mate_copies(e_all.at[0], 1, q))
        side_start()

        @pl.loop(0, tiles)
        def _(i):
            pregrad(0, i, "own")

        @pl.when(jnp.logical_not(first))
        def _():
            start(dot_copies())

    def pass_back(q, shift):
        total = b_send[my_rows, columns(q)].astype(jnp.float32)
        for j, copy in enumerate(sum_copies(b_send, b_recv, 1, q)):
            copy.wait()
            total += b_recv[j, :, columns(q)].astype(jnp.float32)
        scale = scale_all[my_rows, 0:1]
        unit = h_all[my_rows, columns(q)].astype(jnp.float32) * scale
        previous = e_all[0, my_rows, columns(q)].astype(jnp.float32) + scale * (
            total * gain_ref[:, columns(q)] - unit * shift
        )
        g_hop[:, columns(q)] = previous.astype(jnp.bfloat16)
        start(backward_hop(q))

    def row_shift():
        total = dot_part[my_rows, :]
        for j in range(parts - 1):
            total += dot_recv[j]
        return jnp.sum(total, axis=1, keepdims=True) * (HALF_BACK / full)

    @pl.loop(0, blocks)
    def _(b):
        total = jnp.zeros((rows, block_width), jnp.float32)
        for i in range(tiles):
            total += lax.dot_general(
                p_all[i, 0:rows, :],
                w1[i, block_columns(b), :],
                CONTRACT_LAST,
                preferred_element_type=jnp.float32,
            )
        total *= 0.5

        @pl.when(jnp.logical_not(first))
        def _():
            b_send[:, block_columns(b)] = total.astype(jnp.bfloat16)
            for t in range(span):
                start(sum_copies(b_send, b_recv, 1, b * span + t))

        unit = h_all[:, block_columns(b)].astype(jnp.float32) * spread(scale_all[...], block_width)
        gain_part[:, block_columns(b)] = jnp.sum(
            (total * unit).reshape(rows // 8, 8, block_width), axis=0
        )

        @pl.when(jnp.logical_not(first))
        def _():
            @pl.when(b == lag)
            def _():
                finish(dot_copies())

            @pl.when(b >= lag)
            def _():
                for t in range(span):
                    pass_back((b - lag) * span + t, row_shift())

        @pl.when(b == min(lag, blocks - 1))
        def _():
            for d in range(1, replicas):
                for copy in side_copies(d):
                    copy.wait_recv()
                start(pass_copies(d))

    @pl.when(jnp.logical_not(first))
    def _():
        for q in range(max(0, blocks - lag) * span, chunks):
            pass_back(q, row_shift())

    gain_copies = [
        remote(
            gain_part.at[:, pl.ds(pl.multiple_of(part * width, width), width)],
            gain_recv.at[d * parts + j],
            gain_ssem.at[d * parts + j],
            gain_rsem.at[d * parts + j],
            {"dp": other, "mp": part},
        )
        for d, j, other, part in peers
    ]
    start(gain_copies)

    @pl.when(last)
    def _():
        replica_forward("last")

    for d in range(1, replicas):
        finish(pass_copies(d))
        for copy in side_copies(d):
            copy.wait_send()
    outs = []
    for d in range(replicas):
        place = pl.ds(d * rows, rows)
        outs.append(
            pltpu.make_async_copy(e_all.at[d, :, kept], e_cols.at[place, :], out_sem.at[d])
        )
    start(outs)
    for d in range(1, replicas):

        @pl.loop(0, tiles)
        def _(i):
            pregrad(d, i, "other")

    total = gain_part[:, my_cols]
    for (d, j, _, _), copy in zip(peers, gain_copies):
        copy.wait()
        total += gain_recv[d * parts + j]
    gain_out[...] = jnp.sum(total, axis=0, keepdims=True)

    finish(outs)

    @pl.when(jnp.logical_not(first))
    def _():
        for q in range(chunks):
            for copy in backward_hop(q):
                copy.wait_send()


def weight_grads(
    u_ref, e_ref, gain_ref, p_ref, zt_ref, in_hbm, out_hbm, gain_out, in_buf, out_buf, in_sem, out_sem
):
    tiles, _, tile = in_buf.shape
    gain_out[...] = gain_ref[...]

    def in_copy(i):
        place = pl.ds(pl.multiple_of(i * tile, tile), tile)
        return pltpu.make_async_copy(in_buf.at[i], in_hbm.at[:, place], in_sem.at[i])

    def out_copy(i):
        place = pl.ds(pl.multiple_of(i * tile, tile), tile)
        return pltpu.make_async_copy(out_buf.at[place], out_hbm.at[place], out_sem.at[i])

    @pl.loop(0, tiles)
    def _(i):
        place = pl.ds(pl.multiple_of(i * tile, tile), tile)
        product = jnp.dot(u_ref[...], p_ref[i], preferred_element_type=jnp.float32)
        in_buf[i] = (product * 0.5).astype(in_buf.dtype)
        in_copy(i).start()
        product = jnp.dot(zt_ref[place], e_ref[...], preferred_element_type=jnp.float32)
        out_buf[place] = (product * HALF_BACK).astype(out_buf.dtype)
        out_copy(i).start()

    @pl.loop(0, tiles)
    def _(i):
        in_copy(i).wait()
        out_copy(i).wait()


def shards(inputs, cotangent, gain, weight_in, weight_out):
    stages = lax.axis_size("pipe")
    parts = lax.axis_size("mp")
    replicas = lax.axis_size("dp")
    micro, row_count, width = inputs.shape
    rows = micro * row_count
    full = gain.shape[1]
    hidden = weight_in.shape[2]
    tile = math.gcd(hidden, 1024)
    tiles = hidden // tile
    own = rows // parts
    chips = parts // 2
    half = full // replicas
    hop_width = math.gcd(full, 128)
    chunks = full // hop_width
    span = math.gcd(chunks, 2)
    lanes = 128
    count = replicas * rows
    kept_bytes = 4 * count * (hidden + half) + 65536
    bf16, f32 = jnp.bfloat16, jnp.float32
    vmem = pl.BlockSpec(memory_space=pltpu.VMEM)
    anywhere = pl.BlockSpec(memory_space=pl.ANY)
    dma = pltpu.SemaphoreType.DMA
    zt_all, p_all, u_flip, e_cols, gain_total = pl.pallas_call(
        functools.partial(relay, (stages, parts, replicas, hop_width, span)),
        name="relay",
        out_shape=(
            pltpu.VMEM((hidden, count), bf16),
            pltpu.VMEM((tiles, count, tile), bf16),
            pltpu.VMEM((half, count), bf16),
            pltpu.VMEM((count, half), bf16),
            pltpu.VMEM((1, width), f32),
        ),
        in_specs=[vmem, vmem, vmem, anywhere, anywhere],
        out_specs=(vmem, vmem, vmem, vmem, vmem),
        scratch_shapes=[
            pltpu.VMEM((tiles, full, tile), bf16),
            pltpu.VMEM((tiles, tile, full), bf16),
            pltpu.VMEM((tiles, rows, tile), bf16),
            pltpu.VMEM((tiles, rows, tile), bf16),
            pltpu.VMEM((rows, full), bf16),
            pltpu.VMEM((replicas, rows, full), bf16),
            pltpu.VMEM((replicas, rows, full), bf16),
            pltpu.VMEM((rows, full), bf16),
            pltpu.VMEM((parts - 1, own, full), bf16),
            pltpu.VMEM((rows, full), bf16),
            pltpu.VMEM((parts - 1, own, full), bf16),
            pltpu.VMEM((own, full), bf16),
            pltpu.VMEM((own, full), bf16),
            pltpu.VMEM((rows, lanes), f32),
            pltpu.VMEM((rows, lanes), f32),
            pltpu.VMEM((rows, lanes), f32),
            pltpu.VMEM((parts - 1, own, lanes), f32),
            pltpu.VMEM((8, full), f32),
            pltpu.VMEM((replicas * parts, 8, width), f32),
            dma((tiles,)),
            dma((tiles,)),
            dma((replicas,)),
            dma((parts,)),
            dma((parts,)),
            dma((2, chunks, chips)),
            dma((2, chunks, chips)),
            dma((2, chunks, chips)),
            dma((2, chunks, chips)),
            dma((replicas, chips)),
            dma((replicas, chips)),
            dma((replicas, chips)),
            dma((replicas, chips)),
            dma((2, replicas)),
            dma((2, replicas)),
            dma((2, chunks, parts)),
            dma((2, chunks, parts)),
            dma((parts,)),
            dma((parts,)),
            dma((replicas * parts,)),
            dma((replicas * parts,)),
        ],
        compiler_params=pltpu.CompilerParams(
            collective_id=0, has_side_effects=True, vmem_limit_bytes=67043328 - kept_bytes
        ),
    )(
        inputs.reshape(rows, width),
        cotangent.reshape(rows, width),
        gain,
        weight_in[0],
        weight_out[0],
    )
    stay = functools.partial(
        pltpu.with_memory_space_constraint, memory_space=pltpu.MemorySpace.VMEM
    )
    grad_first, grad_second, gain_sum = pl.pallas_call(
        weight_grads,
        name="weight_grads",
        out_shape=(
            jax.ShapeDtypeStruct((half, hidden), bf16),
            jax.ShapeDtypeStruct((hidden, half), bf16),
            jax.ShapeDtypeStruct((1, width), f32),
        ),
        in_specs=[vmem, vmem, vmem, vmem, vmem],
        out_specs=(anywhere, anywhere, vmem),
        scratch_shapes=[
            pltpu.VMEM((tiles, half, tile), bf16),
            pltpu.VMEM((hidden, half), bf16),
            dma((tiles,)),
            dma((tiles,)),
        ],
        compiler_params=pltpu.CompilerParams(vmem_limit_bytes=67043328 - kept_bytes),
    )(*(stay(array) for array in (u_flip, e_cols, gain_total, p_all, zt_all)))
    return (grad_first[None], grad_second[None], gain_sum)


def solution(mesh):
    in_specs = (
        P(None, "dp", "mp"),
        P(None, "dp", "mp"),
        P("pipe", None),
        P("pipe", None, "mp"),
        P("pipe", "mp", None),
    )
    out_specs = (P("pipe", "dp", "mp"), P("pipe", "mp", "dp"), P("pipe", "mp"))
    return jax.shard_map(shards, mesh=mesh, in_specs=in_specs, out_specs=out_specs, check_vma=False)
```

```python
import functools
import math

import jax
import jax.numpy as jnp
from jax import lax
from jax.experimental import pallas as pl
from jax.experimental.pallas import tpu as pltpu
from jax.sharding import PartitionSpec as P

GELU_COEF = math.sqrt(2.0 / math.pi)
CUBIC_COEF = 0.044715
NORM_EPS = 1e-06
CONTRACT_LAST = (((1,), (1,)), ((), ()))
MESH = pl.DeviceIdType.MESH


CUBE = CUBIC_COEF / (GELU_COEF * GELU_COEF)
HALF_BACK = 0.5 / GELU_COEF


def gelu_tanh(y):
    bent = y * (CUBE * (y * y))
    return (bent, jnp.tanh(y + bent))


def gelu_value(y, tangent):
    return y * (1.0 + tangent)


def gelu_slope(y, bent, tangent):
    above = 1.0 + tangent
    return above + (1.0 - tangent) * above * (y + 3.0 * bent)


def relay(
    sizes,
    x_ref,
    cot_ref,
    gain_ref,
    w1_hbm,
    w2_hbm,
    zt_all,
    p_all,
    ut,
    e_cols,
    gain_out,
    w1,
    w2,
    z_keep,
    a_keep,
    h_all,
    u_all,
    e_all,
    sums,
    f_recv,
    b_recv,
    h_hop,
    g_hop,
    scale_all,
    bend_all,
    dot_part,
    dot_recv,
    gain_part,
    gain_recv,
    w1_sem,
    w2_sem,
    out_sem,
    x_ssem,
    x_rsem,
    hop_ssem,
    hop_rsem,
    mate_ssem,
    mate_rsem,
    side_ssem,
    side_rsem,
    pass_ssem,
    pass_rsem,
    u_ssem,
    u_rsem,
    rs_ssem,
    rs_rsem,
    dot_ssem,
    dot_rsem,
    gain_ssem,
    gain_rsem,
):
    stages, parts, replicas, hop_width, span = sizes
    sec = lax.axis_index("pipe")
    me = lax.axis_index("mp")
    rep = lax.axis_index("dp")
    tiles, full, tile = w1.shape
    rows = h_all.shape[0]
    own = rows // parts
    width = full // parts
    chunks = full // hop_width
    lag = 2
    first = sec == 0
    last = sec == stages - 1
    chips = parts // 2
    chip, core = me // 2, lax.rem(me, 2)
    mate = chip * 2 + 1 - core

    def w_copies(i):
        start = pl.multiple_of(i * tile, tile)
        return (
            pltpu.make_async_copy(w1_hbm.at[:, pl.ds(start, tile)], w1.at[i], w1_sem.at[i]),
            pltpu.make_async_copy(w2_hbm.at[pl.ds(start, tile), :], w2.at[i], w2_sem.at[i]),
        )

    for which in range(2):
        for i in range(tiles):
            w_copies(i)[which].start()

    def across_core(k):
        return lax.rem(chip + k, chips) * 2 + 1 - core

    barrier = pltpu.get_barrier_semaphore()
    peers = []
    for d in range(replicas):
        for j in range(parts):
            if d or j:
                peers.append((d, j, lax.rem(rep + d, replicas), lax.rem(me + j, parts)))
    for _, _, other, part in peers:
        pl.semaphore_signal(
            barrier, inc=1, device_id={"dp": other, "mp": part}, device_id_type=MESH
        )
    for step in (1, stages - 1):
        for k in range(chips):
            pl.semaphore_signal(
                barrier,
                inc=1,
                device_id={"pipe": lax.rem(sec + step, stages), "mp": across_core(k)},
                device_id_type=MESH,
            )
    dot_part[...] = jnp.zeros_like(dot_part)
    pl.semaphore_wait(barrier, len(peers) + 2 * chips)

    my_rows = pl.ds(pl.multiple_of(me * own, own), own)
    my_cols = pl.ds(pl.multiple_of(me * width, width), width)

    half = full // replicas
    kept = pl.ds(pl.multiple_of(rep * half, half), half)

    def remote(src, dst, ssem, rsem, where):
        return pltpu.make_async_remote_copy(
            src_ref=src,
            dst_ref=dst,
            send_sem=ssem,
            recv_sem=rsem,
            device_id=where,
            device_id_type=MESH,
        )

    def others():
        return [(j, lax.rem(me + j, parts)) for j in range(1, parts)]

    def columns(q):
        return pl.ds(pl.multiple_of(q * hop_width, hop_width), hop_width)

    blocks = chunks // span
    block_width = hop_width * span

    def block_columns(b):
        return pl.ds(pl.multiple_of(b * block_width, block_width), block_width)

    def start(copies):
        for copy in copies:
            copy.start()

    def finish(copies):
        for copy in copies:
            copy.wait()

    def block_rows(k):
        block = lax.rem(chip + chips - k, chips) * 2 + 1 - core
        return pl.ds(pl.multiple_of(block * own, own), own)

    def hop_copies(src, dst, which, q, step):
        return [
            remote(
                src.at[:, columns(q)],
                dst.at[my_rows, columns(q)],
                hop_ssem.at[which],
                hop_rsem.at[which, q],
                {"pipe": lax.rem(sec + step, stages), "mp": across_core(k)},
            )
            for k in range(chips)
        ]

    def forward_hop(q):
        return hop_copies(h_hop, h_all, 0, q, 1)

    def backward_hop(q):
        return hop_copies(g_hop, e_all.at[0], 1, q, stages - 1)

    def arrived(ref, sem):
        pltpu.make_async_copy(ref, ref, sem).wait()

    def block_bytes(ref, count, cols=slice(None)):
        return ref.at[pl.ds(0, count * own), cols]

    def hop_arrived(ref, which, q):
        arrived(block_bytes(ref, chips, columns(q)), hop_rsem.at[which, q])

    def mate_arrived(ref, which, q):
        arrived(block_bytes(ref, chips, columns(q)), mate_rsem.at[which, q])

    def sums_arrived(recv, which, q):
        arrived(recv.at[:, :, columns(q)], rs_rsem.at[which, q])

    def sent(which):
        arrived(block_bytes(h_all, chips), hop_ssem.at[which])
        arrived(block_bytes(h_all, parts - 1), rs_ssem.at[which])

    def mate_copies(ref, which, q):
        copies = []
        for k in range(chips):
            part = ref.at[block_rows(k), columns(q)]
            copies.append(
                remote(part, part, mate_ssem.at[which], mate_rsem.at[which, q], {"mp": mate})
            )
        return copies

    def side_copies(d):
        return [
            remote(
                e_all.at[0, block_rows(k)],
                e_all.at[d, block_rows(k)],
                side_ssem.at[d],
                side_rsem.at[d],
                {"dp": lax.rem(rep + d, replicas)},
            )
            for k in range(chips)
        ]

    def pass_copies(d):
        copies = []
        for k in range(chips):
            part = e_all.at[d, block_rows(k)]
            copies.append(
                remote(part, part, pass_ssem.at[d], pass_rsem.at[d], {"mp": mate})
            )
        return copies

    def u_copies(d):
        part = pl.ds(pl.multiple_of(core * (rows // 2), rows // 2), rows // 2)
        there = {"dp": lax.rem(rep + d, replicas)}
        return (
            remote(u_all.at[0, part], u_all.at[d, part], u_ssem.at[0, d], u_rsem.at[0, d], there),
            remote(
                u_all.at[d, part], u_all.at[d, part], u_ssem.at[1, d], u_rsem.at[1, d], {"mp": mate}
            ),
        )

    def gather_features(src, dst):
        def cols(k):
            block = lax.rem(chip + chips - k, chips) * 2 + core
            return pl.ds(pl.multiple_of(block * width, width), width)

        def across(k):
            target = lax.rem(chip + k, chips) * 2 + core
            return remote(src, dst.at[:, my_cols], x_ssem.at[k], x_rsem.at[k], {"mp": target})

        def beside(k):
            part = dst.at[:, cols(k)]
            slot = chips + k
            return remote(
                src if k == 0 else part, part, x_ssem.at[slot], x_rsem.at[slot], {"mp": mate}
            )

        for k in range(1, chips):
            across(k).start()
        beside(0).start()
        dst[:, my_cols] = src[...]
        for k in range(1, chips):
            across(k).wait_recv()
            beside(k).start()
        for k in range(1, chips):
            across(k).wait_send()
        for k in range(chips):
            beside(k).wait()

    def sum_copies(src, dst, which, q):
        return [
            remote(
                src.at[pl.ds(pl.multiple_of(part * own, own), own), columns(q)],
                dst.at[j - 1, :, columns(q)],
                rs_ssem.at[which],
                rs_rsem.at[which, q],
                {"mp": part},
            )
            for j, part in others()
        ]

    def dot_copies():
        return [
            remote(
                dot_part.at[pl.ds(pl.multiple_of(part * own, own), own)],
                dot_recv.at[j - 1],
                dot_ssem.at[j],
                dot_rsem.at[j],
                {"mp": part},
            )
            for j, part in others()
        ]

    early = min(5, tiles)
    part_width = chunks // 2 * hop_width
    step_width = math.gcd(tile, 256)
    steps = tile // step_width
    lanes = scale_all.shape[1]

    def staged(product, use):
        held = product(0)
        for s in range(1, steps):
            ahead = product(s)
            use(s - 1, held)
            held = ahead
        use(steps - 1, held)

    def fold(values):
        total = values[:, :lanes]
        for c in range(lanes, values.shape[1], lanes):
            total += values[:, c : c + lanes]
        return total

    def spread(values, count):
        return jnp.concatenate([values] * (count // lanes), axis=1)

    def spot(d, i, s):
        return i, slice(d * rows, (d + 1) * rows), slice(s * step_width, (s + 1) * step_width)

    def activate(d, i, kind, rest=False):
        begin = part_width if rest else 0

        def product(s):
            piece = w1[i, begin:, s * step_width : (s + 1) * step_width]
            return jnp.dot(u_all[d, :, begin:], piece, preferred_element_type=jnp.float32)

        def use(s, gate):
            place = slice(s * step_width, (s + 1) * step_width)
            if rest:
                gate += z_keep[i, :, place].astype(jnp.float32)
            if kind == "other":
                y = (gate * GELU_COEF).astype(jnp.bfloat16)
            else:
                y = (gate * spread(bend_all[...], step_width)).astype(jnp.bfloat16)
                a_keep[i, :, place] = y
            bent, tangent = gelu_tanh(y)
            if kind != "last":
                z_keep[i, :, place] = gelu_value(y, tangent)
            if kind != "own":
                slope = gelu_slope(y, bent, tangent)
                if kind == "last":
                    slope = slope * p_all[spot(d, i, s)]
                    dot_part[...] += fold((slope * y).astype(jnp.float32))
                p_all[spot(d, i, s)] = slope

        staged(product, use)

    def complete(i, kind):
        for s in range(steps):
            place = slice(s * step_width, (s + 1) * step_width)
            y = a_keep[i, :, place].astype(jnp.float32)
            bent, tangent = gelu_tanh(y)
            if kind == "own":
                p_all[spot(0, i, s)] = gelu_slope(y, bent, tangent).astype(jnp.bfloat16)
            else:
                z_keep[i, :, place] = gelu_value(y, tangent).astype(jnp.bfloat16)

    def pregrad(d, i, kind, rest=False):
        begin = part_width if rest else 0

        def product(s):
            piece = w2[i, s * step_width : (s + 1) * step_width, begin:]
            return lax.dot_general(
                e_all[d, :, begin:], piece, CONTRACT_LAST, preferred_element_type=jnp.float32
            )

        def use(s, inner):
            place = slice(s * step_width, (s + 1) * step_width)
            if rest:
                inner += z_keep[i, :, place].astype(jnp.float32)
            if kind != "plain":
                inner = inner * p_all[spot(d, i, s)].astype(jnp.float32)
            if kind == "own":
                dot_part[...] += fold(inner * a_keep[i, :, place].astype(jnp.float32))
            p_all[spot(d, i, s)] = inner.astype(jnp.bfloat16)

        staged(product, use)

    def turn(d, i):
        for s in range(steps):
            place = slice(s * step_width, (s + 1) * step_width)
            down = pl.ds(pl.multiple_of(i * tile + s * step_width, step_width), step_width)
            flipped = z_keep[i, :, place].astype(jnp.float32).T
            zt_all[down, d * rows : (d + 1) * rows] = flipped.astype(jnp.bfloat16)

    def side_start():
        for d in range(1, replicas):
            start(side_copies(d))

    @pl.when(last)
    def _():
        gather_features(cot_ref, e_all.at[0])
        side_start()

        @pl.loop(0, tiles)
        def _(i):
            w_copies(i)[1].wait()
            pregrad(0, i, "plain")

    def mates_sent(ref, which):
        arrived(block_bytes(ref, chips), mate_ssem.at[which])

    def receive(ref, which, begin, end):
        @pl.loop(begin, end)
        def _(q):
            hop_arrived(ref, which, q)
            start(mate_copies(ref, which, q))

    def between(ref, which, work):
        @pl.loop(0, early)
        def _(i):
            work(i)

            @pl.when(i < chunks - chunks // 2)
            def _():
                q = chunks // 2 + i
                hop_arrived(ref, which, q)
                start(mate_copies(ref, which, q))

        receive(ref, which, chunks // 2 + min(early, chunks - chunks // 2), chunks)

    def activate_early(i):
        w_copies(i)[0].wait()

        def product(s):
            piece = w1[i, :part_width, s * step_width : (s + 1) * step_width]
            return jnp.dot(u_all[0, :, :part_width], piece, preferred_element_type=jnp.float32)

        def use(s, gate):
            z_keep[i, :, s * step_width : (s + 1) * step_width] = gate.astype(jnp.bfloat16)

        staged(product, use)

    def pregrad_early(i):
        def product(s):
            piece = w2[i, s * step_width : (s + 1) * step_width, :part_width]
            return lax.dot_general(
                e_all[0, :, :part_width], piece, CONTRACT_LAST, preferred_element_type=jnp.float32
            )

        def use(s, inner):
            z_keep[i, :, s * step_width : (s + 1) * step_width] = inner.astype(jnp.bfloat16)

        staged(product, use)

    def prepare(cols):
        values = h_all[:, cols].astype(jnp.float32)
        u_all[0, :, cols] = (values * gain_ref[:, cols]).astype(jnp.bfloat16)
        return fold(values * values)

    def close(squares):
        scale = lax.rsqrt(jnp.sum(squares, axis=1, keepdims=True) / full + NORM_EPS)
        scale_all[...] = jnp.broadcast_to(scale, scale_all.shape)
        bend_all[...] = scale_all[...] * GELU_COEF

    @pl.when(first)
    def _():
        gather_features(x_ref, h_all)
        squares = prepare(slice(0, hop_width))
        for q in range(1, chunks):
            squares += prepare(slice(q * hop_width, (q + 1) * hop_width))
        close(squares)

    @pl.when(jnp.logical_not(first))
    def _():
        squares = jnp.zeros((rows, lanes), jnp.float32)
        receive(h_all, 0, 0, chunks // 2)
        for q in range(chunks // 2):
            mate_arrived(h_all, 0, q)
            squares += prepare(slice(q * hop_width, (q + 1) * hop_width))
        dot_part[...] = squares
        between(h_all, 0, activate_early)
        squares = dot_part[...]
        for q in range(chunks // 2, chunks):
            mate_arrived(h_all, 0, q)
            squares += prepare(slice(q * hop_width, (q + 1) * hop_width))
        close(squares)
        dot_part[...] = jnp.zeros_like(dot_part)
        mates_sent(h_all, 0)

    def normed():
        values = h_all[...].astype(jnp.float32)
        u_all[0] = (values * scale_all[:, 0:1] * gain_ref[...]).astype(jnp.bfloat16)
        for d in range(1, replicas):
            u_copies(d)[0].start()

    @pl.when(last)
    def _():
        @pl.loop(0, early)
        def _(i):
            activate(0, i, "last", rest=True)

        @pl.loop(early, tiles)
        def _(i):
            w_copies(i)[0].wait()
            activate(0, i, "last")

        start(dot_copies())

    def stream(partial, send, factor, recv, which, pass_block, sending):
        @pl.loop(0, blocks)
        def _(b):
            send[:, block_columns(b)] = (partial(b) * factor).astype(jnp.bfloat16)

            @pl.when(sending)
            def _():
                for t in range(span):
                    start(sum_copies(send, recv, which, b * span + t))

            @pl.when(jnp.logical_and(b >= lag, sending))
            def _():
                pass_block(b - lag)

        @pl.when(sending)
        def _():
            @pl.loop(max(0, blocks - lag), blocks)
            def _(b):
                pass_block(b)

    def pass_on(q):
        total = h_all[my_rows, columns(q)].astype(jnp.float32)
        total += sums[my_rows, columns(q)].astype(jnp.float32)
        sums_arrived(f_recv, 0, q)
        for j in range(parts - 1):
            total += f_recv[j, :, columns(q)].astype(jnp.float32)
        h_hop[:, columns(q)] = total.astype(jnp.bfloat16)
        start(forward_hop(q))

    @pl.when(jnp.logical_not(last))
    def _():
        @pl.when(first)
        def _():
            @pl.loop(0, tiles)
            def _(i):
                w_copies(i)[0].wait()
                activate(0, i, "own")

        @pl.when(jnp.logical_not(first))
        def _():
            @pl.loop(0, early)
            def _(i):
                activate(0, i, "own", rest=True)

            @pl.loop(early, tiles)
            def _(i):
                w_copies(i)[0].wait()
                activate(0, i, "own")

        @pl.loop(0, tiles)
        def _(i):
            w_copies(i)[1].wait()

        def partial(b):
            total = jnp.zeros((rows, block_width), jnp.float32)
            for i in range(tiles):
                total += jnp.dot(
                    z_keep[i], w2[i, :, block_columns(b)], preferred_element_type=jnp.float32
                )
            return total

        def pass_block(b):
            for t in range(span):
                pass_on(b * span + t)

        stream(partial, sums, HALF_BACK, f_recv, 0, pass_block, True)

    def replica_forward(kind):
        normed()

        @pl.loop(0, tiles)
        def _(i):
            complete(i, kind)
            turn(0, i)

        for d in range(1, replicas):
            u_copies(d)[0].wait_recv()
            u_copies(d)[1].start()
        flip_u(0)
        for d in range(1, replicas):
            u_copies(d)[1].wait()
            u_copies(d)[0].wait_send()

            @pl.loop(0, tiles)
            def _(i):
                activate(d, i, "other")
                turn(d, i)

            flip_u(d)

    def flip_u(d):
        flipped = u_all[d, :, kept].astype(jnp.float32).T
        ut[:, d * rows : (d + 1) * rows] = flipped.astype(jnp.bfloat16)

    @pl.when(jnp.logical_not(last))
    def _():
        replica_forward("own")
        sent(0)
        receive(e_all.at[0], 1, 0, chunks // 2)
        for q in range(chunks // 2):
            mate_arrived(e_all.at[0], 1, q)
        between(e_all.at[0], 1, pregrad_early)
        for q in range(chunks // 2, chunks):
            mate_arrived(e_all.at[0], 1, q)
        side_start()
        mates_sent(e_all.at[0], 1)

        @pl.loop(0, early)
        def _(i):
            pregrad(0, i, "own", rest=True)

        @pl.loop(early, tiles)
        def _(i):
            pregrad(0, i, "own")

        @pl.when(jnp.logical_not(first))
        def _():
            start(dot_copies())

    def pass_back(q, shift):
        total = sums[my_rows, columns(q)].astype(jnp.float32)
        sums_arrived(b_recv, 1, q)
        for j in range(parts - 1):
            total += b_recv[j, :, columns(q)].astype(jnp.float32)
        scale = scale_all[my_rows, 0:1]
        unit = h_all[my_rows, columns(q)].astype(jnp.float32) * scale
        previous = e_all[0, my_rows, columns(q)].astype(jnp.float32) + scale * (
            total * gain_ref[:, columns(q)] - unit * shift
        )
        g_hop[:, columns(q)] = previous.astype(jnp.bfloat16)
        start(backward_hop(q))

    def row_shift():
        total = dot_part[my_rows, :]
        for j in range(parts - 1):
            total += dot_recv[j]
        return jnp.sum(total, axis=1, keepdims=True) * (HALF_BACK / full)

    def partial(b):
        total = jnp.zeros((rows, block_width), jnp.float32)
        for i in range(tiles):
            total += lax.dot_general(
                p_all[i, 0:rows, :],
                w1[i, block_columns(b), :],
                CONTRACT_LAST,
                preferred_element_type=jnp.float32,
            )
        return total

    def pass_block(b):
        @pl.when(b == 0)
        def _():
            finish(dot_copies())

        for t in range(span):
            pass_back(b * span + t, row_shift())

    stream(partial, sums, 0.5, b_recv, 1, pass_block, jnp.logical_not(first))

    for d in range(1, replicas):
        arrived(block_bytes(e_all.at[d], chips), side_rsem.at[d])
        start(pass_copies(d))

    @pl.loop(0, blocks)
    def _(b):
        unit = h_all[:, block_columns(b)].astype(jnp.float32) * spread(scale_all[...], block_width)
        terms = sums[:, block_columns(b)].astype(jnp.float32) * unit
        gain_part[:, block_columns(b)] = jnp.sum(terms.reshape(rows // 8, 8, block_width), axis=0)

    gain_copies = [
        remote(
            gain_part.at[:, pl.ds(pl.multiple_of(part * width, width), width)],
            gain_recv.at[d * parts + j],
            gain_ssem.at[d * parts + j],
            gain_rsem.at[d * parts + j],
            {"dp": other, "mp": part},
        )
        for d, j, other, part in peers
    ]
    start(gain_copies)

    @pl.when(last)
    def _():
        replica_forward("last")

    for d in range(1, replicas):
        arrived(block_bytes(e_all.at[d], chips), pass_rsem.at[d])
        arrived(block_bytes(e_all.at[d], chips), pass_ssem.at[d])
        arrived(block_bytes(e_all.at[d], chips), side_ssem.at[d])
    outs = []
    for d in range(replicas):
        place = pl.ds(d * rows, rows)
        outs.append(
            pltpu.make_async_copy(e_all.at[d, :, kept], e_cols.at[place, :], out_sem.at[d])
        )
    start(outs)
    for d in range(1, replicas):

        @pl.loop(0, tiles)
        def _(i):
            pregrad(d, i, "other")

    total = gain_part[:, my_cols]
    for (d, j, _, _), copy in zip(peers, gain_copies):
        copy.wait()
        total += gain_recv[d * parts + j]
    gain_out[...] = jnp.sum(total, axis=0, keepdims=True)

    finish(outs)

    @pl.when(jnp.logical_not(first))
    def _():
        sent(1)


def weight_grads(
    u_ref, e_ref, gain_ref, p_ref, zt_ref, in_hbm, out_hbm, gain_out, in_buf, out_buf, in_sem, out_sem
):
    tiles, _, tile = in_buf.shape
    gain_out[...] = gain_ref[...]

    def in_copy(i):
        place = pl.ds(pl.multiple_of(i * tile, tile), tile)
        return pltpu.make_async_copy(in_buf.at[i], in_hbm.at[:, place], in_sem.at[i])

    def out_copy(i):
        place = pl.ds(pl.multiple_of(i * tile, tile), tile)
        return pltpu.make_async_copy(out_buf.at[place], out_hbm.at[place], out_sem.at[i])

    @pl.loop(0, tiles)
    def _(i):
        place = pl.ds(pl.multiple_of(i * tile, tile), tile)
        product = jnp.dot(u_ref[...], p_ref[i], preferred_element_type=jnp.float32)
        in_buf[i] = (product * 0.5).astype(in_buf.dtype)
        in_copy(i).start()
        product = jnp.dot(zt_ref[place], e_ref[...], preferred_element_type=jnp.float32)
        out_buf[place] = (product * HALF_BACK).astype(out_buf.dtype)
        out_copy(i).start()

    @pl.loop(0, tiles)
    def _(i):
        in_copy(i).wait()
        out_copy(i).wait()


def shards(inputs, cotangent, gain, weight_in, weight_out):
    stages = lax.axis_size("pipe")
    parts = lax.axis_size("mp")
    replicas = lax.axis_size("dp")
    micro, row_count, width = inputs.shape
    rows = micro * row_count
    full = gain.shape[1]
    hidden = weight_in.shape[2]
    tile = math.gcd(hidden, 1024)
    tiles = hidden // tile
    own = rows // parts
    chips = parts // 2
    half = full // replicas
    hop_width = math.gcd(full, 128)
    chunks = full // hop_width
    span = math.gcd(chunks, 2)
    lanes = 128
    count = replicas * rows
    kept_bytes = 4 * count * (hidden + half) + 65536
    bf16, f32 = jnp.bfloat16, jnp.float32
    vmem = pl.BlockSpec(memory_space=pltpu.VMEM)
    anywhere = pl.BlockSpec(memory_space=pl.ANY)
    dma = pltpu.SemaphoreType.DMA
    zt_all, p_all, u_flip, e_cols, gain_total = pl.pallas_call(
        functools.partial(relay, (stages, parts, replicas, hop_width, span)),
        name="relay",
        out_shape=(
            pltpu.VMEM((hidden, count), bf16),
            pltpu.VMEM((tiles, count, tile), bf16),
            pltpu.VMEM((half, count), bf16),
            pltpu.VMEM((count, half), bf16),
            pltpu.VMEM((1, width), f32),
        ),
        in_specs=[vmem, vmem, vmem, anywhere, anywhere],
        out_specs=(vmem, vmem, vmem, vmem, vmem),
        scratch_shapes=[
            pltpu.VMEM((tiles, full, tile), bf16),
            pltpu.VMEM((tiles, tile, full), bf16),
            pltpu.VMEM((tiles, rows, tile), bf16),
            pltpu.VMEM((tiles, rows, tile), bf16),
            pltpu.VMEM((rows, full), bf16),
            pltpu.VMEM((replicas, rows, full), bf16),
            pltpu.VMEM((replicas, rows, full), bf16),
            pltpu.VMEM((rows, full), bf16),
            pltpu.VMEM((parts - 1, own, full), bf16),
            pltpu.VMEM((parts - 1, own, full), bf16),
            pltpu.VMEM((own, full), bf16),
            pltpu.VMEM((own, full), bf16),
            pltpu.VMEM((rows, lanes), f32),
            pltpu.VMEM((rows, lanes), f32),
            pltpu.VMEM((rows, lanes), f32),
            pltpu.VMEM((parts - 1, own, lanes), f32),
            pltpu.VMEM((8, full), f32),
            pltpu.VMEM((replicas * parts, 8, width), f32),
            dma((tiles,)),
            dma((tiles,)),
            dma((replicas,)),
            dma((parts,)),
            dma((parts,)),
            dma((2,)),
            dma((2, chunks)),
            dma((2,)),
            dma((2, chunks)),
            dma((replicas,)),
            dma((replicas,)),
            dma((replicas,)),
            dma((replicas,)),
            dma((2, replicas)),
            dma((2, replicas)),
            dma((2,)),
            dma((2, chunks)),
            dma((parts,)),
            dma((parts,)),
            dma((replicas * parts,)),
            dma((replicas * parts,)),
        ],
        compiler_params=pltpu.CompilerParams(
            collective_id=0, has_side_effects=True, vmem_limit_bytes=67043328 - kept_bytes
        ),
    )(
        inputs.reshape(rows, width),
        cotangent.reshape(rows, width),
        gain,
        weight_in[0],
        weight_out[0],
    )
    stay = functools.partial(
        pltpu.with_memory_space_constraint, memory_space=pltpu.MemorySpace.VMEM
    )
    grad_first, grad_second, gain_sum = pl.pallas_call(
        weight_grads,
        name="weight_grads",
        out_shape=(
            jax.ShapeDtypeStruct((half, hidden), bf16),
            jax.ShapeDtypeStruct((hidden, half), bf16),
            jax.ShapeDtypeStruct((1, width), f32),
        ),
        in_specs=[vmem, vmem, vmem, vmem, vmem],
        out_specs=(anywhere, anywhere, vmem),
        scratch_shapes=[
            pltpu.VMEM((tiles, half, tile), bf16),
            pltpu.VMEM((hidden, half), bf16),
            dma((tiles,)),
            dma((tiles,)),
        ],
        compiler_params=pltpu.CompilerParams(vmem_limit_bytes=67043328 - kept_bytes),
    )(*(stay(array) for array in (u_flip, e_cols, gain_total, p_all, zt_all)))
    return (grad_first[None], grad_second[None], gain_sum)


def solution(mesh):
    in_specs = (
        P(None, "dp", "mp"),
        P(None, "dp", "mp"),
        P("pipe", None),
        P("pipe", None, "mp"),
        P("pipe", "mp", None),
    )
    out_specs = (P("pipe", "dp", "mp"), P("pipe", "mp", "dp"), P("pipe", "mp"))
    return jax.shard_map(shards, mesh=mesh, in_specs=in_specs, out_specs=out_specs, check_vma=False)
```

```python
import functools
import math

import jax
import jax.numpy as jnp
from jax import lax
from jax.experimental import pallas as pl
from jax.experimental.pallas import tpu as pltpu
from jax.sharding import PartitionSpec as P

GELU_COEF = math.sqrt(2.0 / math.pi)
CUBIC_COEF = 0.044715
NORM_EPS = 1e-06
CONTRACT_LAST = (((1,), (1,)), ((), ()))
MESH = pl.DeviceIdType.MESH


CUBE = CUBIC_COEF / (GELU_COEF * GELU_COEF)
HALF_BACK = 0.5 / GELU_COEF


def gelu_tanh(y):
    bent = y * (CUBE * (y * y))
    return (bent, jnp.tanh(y + bent))


def gelu_value(y, tangent):
    return y * (1.0 + tangent)


def gelu_slope(y, bent, tangent):
    above = 1.0 + tangent
    return above + (1.0 - tangent) * above * (y + 3.0 * bent)


def relay(
    sizes,
    x_ref,
    cot_ref,
    gain_ref,
    w1_hbm,
    w2_hbm,
    zt_all,
    p_all,
    ut,
    e_cols,
    gain_out,
    w1,
    w2,
    z_keep,
    a_keep,
    h_all,
    u_all,
    e_all,
    sums,
    f_recv,
    b_recv,
    h_hop,
    g_hop,
    scale_all,
    bend_all,
    dot_part,
    dot_recv,
    gain_part,
    gain_recv,
    w1_sem,
    w2_sem,
    out_sem,
    x_ssem,
    x_rsem,
    hop_ssem,
    hop_rsem,
    mate_ssem,
    mate_rsem,
    side_ssem,
    side_rsem,
    pass_ssem,
    pass_rsem,
    u_ssem,
    u_rsem,
    rs_ssem,
    rs_rsem,
    dot_ssem,
    dot_rsem,
    gain_ssem,
    gain_rsem,
):
    stages, parts, replicas, hop_width, span = sizes
    sec = lax.axis_index("pipe")
    me = lax.axis_index("mp")
    rep = lax.axis_index("dp")
    tiles, full, tile = w1.shape
    rows = h_all.shape[0]
    own = rows // parts
    width = full // parts
    chunks = full // hop_width
    lag = 2
    first = sec == 0
    last = sec == stages - 1
    chips = parts // 2
    chip, core = me // 2, lax.rem(me, 2)
    mate = chip * 2 + 1 - core

    def w_copies(i):
        start = pl.multiple_of(i * tile, tile)
        return (
            pltpu.make_async_copy(w1_hbm.at[:, pl.ds(start, tile)], w1.at[i], w1_sem.at[i]),
            pltpu.make_async_copy(w2_hbm.at[pl.ds(start, tile), :], w2.at[i], w2_sem.at[i]),
        )

    def fetch(which):
        for i in range(tiles):
            w_copies(i)[which].start()

    fetch(0)

    def across_core(k):
        return lax.rem(chip + k, chips) * 2 + 1 - core

    barrier = pltpu.get_barrier_semaphore()
    peers = []
    for d in range(replicas):
        for j in range(parts):
            if d or j:
                peers.append((d, j, lax.rem(rep + d, replicas), lax.rem(me + j, parts)))
    for _, _, other, part in peers:
        pl.semaphore_signal(
            barrier, inc=1, device_id={"dp": other, "mp": part}, device_id_type=MESH
        )
    for there, absent in ((sec + 1, last), (sec - 1, first)):

        @pl.when(jnp.logical_not(absent))
        def _():
            for k in range(chips):
                pl.semaphore_signal(
                    barrier,
                    inc=1,
                    device_id={"pipe": there, "mp": across_core(k)},
                    device_id_type=MESH,
                )

    neighbours = 2 - first.astype(jnp.int32) - last.astype(jnp.int32)
    dot_part[...] = jnp.zeros_like(dot_part)
    pl.semaphore_wait(barrier, len(peers) + chips * neighbours)

    pl.when(jnp.logical_not(first))(lambda: fetch(1))

    my_rows = pl.ds(pl.multiple_of(me * own, own), own)
    my_cols = pl.ds(pl.multiple_of(me * width, width), width)

    half = full // replicas
    kept = pl.ds(pl.multiple_of(rep * half, half), half)

    def remote(src, dst, ssem, rsem, where):
        return pltpu.make_async_remote_copy(
            src_ref=src,
            dst_ref=dst,
            send_sem=ssem,
            recv_sem=rsem,
            device_id=where,
            device_id_type=MESH,
        )

    def others():
        return [(j, lax.rem(me + j, parts)) for j in range(1, parts)]

    def columns(q):
        return pl.ds(pl.multiple_of(q * hop_width, hop_width), hop_width)

    blocks = chunks // span
    block_width = hop_width * span

    def block_columns(b):
        return pl.ds(pl.multiple_of(b * block_width, block_width), block_width)

    def start(copies):
        for copy in copies:
            copy.start()

    def finish(copies):
        for copy in copies:
            copy.wait()

    def block_rows(k):
        block = lax.rem(chip + chips - k, chips) * 2 + 1 - core
        return pl.ds(pl.multiple_of(block * own, own), own)

    def hop_copies(src, dst, which, q, step):
        return [
            remote(
                src.at[:, columns(q)],
                dst.at[my_rows, columns(q)],
                hop_ssem.at[which],
                hop_rsem.at[which, q],
                {"pipe": lax.rem(sec + step, stages), "mp": across_core(k)},
            )
            for k in range(chips)
        ]

    def forward_hop(q):
        return hop_copies(h_hop, h_all, 0, q, 1)

    def backward_hop(q):
        return hop_copies(g_hop, e_all.at[0], 1, q, stages - 1)

    def arrived(ref, sem):
        pltpu.make_async_copy(ref, ref, sem).wait()

    def block_bytes(ref, count, cols=slice(None)):
        return ref.at[pl.ds(0, count * own), cols]

    def hop_arrived(ref, which, q):
        arrived(block_bytes(ref, chips, columns(q)), hop_rsem.at[which, q])

    def mate_arrived(ref, which, q):
        arrived(block_bytes(ref, chips, columns(q)), mate_rsem.at[which, q])

    def sums_arrived(recv, which, q):
        arrived(recv.at[:, :, columns(q)], rs_rsem.at[which, q])

    def sent(which):
        arrived(block_bytes(h_all, chips), hop_ssem.at[which])
        arrived(block_bytes(h_all, parts - 1), rs_ssem.at[which])

    def mate_copies(ref, which, q):
        copies = []
        for k in range(chips):
            part = ref.at[block_rows(k), columns(q)]
            copies.append(
                remote(part, part, mate_ssem.at[which], mate_rsem.at[which, q], {"mp": mate})
            )
        return copies

    def side_copies(d):
        return [
            remote(
                e_all.at[0, block_rows(k)],
                e_all.at[d, block_rows(k)],
                side_ssem.at[d],
                side_rsem.at[d],
                {"dp": lax.rem(rep + d, replicas)},
            )
            for k in range(chips)
        ]

    def pass_copies(d):
        copies = []
        for k in range(chips):
            part = e_all.at[d, block_rows(k)]
            copies.append(
                remote(part, part, pass_ssem.at[d], pass_rsem.at[d], {"mp": mate})
            )
        return copies

    def u_copies(d):
        part = pl.ds(pl.multiple_of(core * (rows // 2), rows // 2), rows // 2)
        there = {"dp": lax.rem(rep + d, replicas)}
        return (
            remote(u_all.at[0, part], u_all.at[d, part], u_ssem.at[0, d], u_rsem.at[0, d], there),
            remote(
                u_all.at[d, part], u_all.at[d, part], u_ssem.at[1, d], u_rsem.at[1, d], {"mp": mate}
            ),
        )

    def gather_features(src, dst, meanwhile=None):
        def cols(k):
            block = lax.rem(chip + chips - k, chips) * 2 + core
            return pl.ds(pl.multiple_of(block * width, width), width)

        def across(k):
            target = lax.rem(chip + k, chips) * 2 + core
            return remote(src, dst.at[:, my_cols], x_ssem.at[k], x_rsem.at[k], {"mp": target})

        def beside(k):
            part = dst.at[:, cols(k)]
            slot = chips + k
            return remote(
                src if k == 0 else part, part, x_ssem.at[slot], x_rsem.at[slot], {"mp": mate}
            )

        for k in range(1, chips):
            across(k).start()
        beside(0).start()
        dst[:, my_cols] = src[...]
        if meanwhile is not None:
            beside(0).wait_recv()
            meanwhile[0]()
        for k in range(1, chips):
            across(k).wait_recv()
            beside(k).start()
        if meanwhile is not None:
            meanwhile[1]()
        for k in range(1, chips):
            across(k).wait_send()
        beside(0).wait_send()
        if meanwhile is None:
            beside(0).wait_recv()
        for k in range(1, chips):
            beside(k).wait()

    def sum_copies(src, dst, which, q):
        return [
            remote(
                src.at[pl.ds(pl.multiple_of(part * own, own), own), columns(q)],
                dst.at[j - 1, :, columns(q)],
                rs_ssem.at[which],
                rs_rsem.at[which, q],
                {"mp": part},
            )
            for j, part in others()
        ]

    def dot_copies():
        return [
            remote(
                dot_part.at[pl.ds(pl.multiple_of(part * own, own), own)],
                dot_recv.at[j - 1],
                dot_ssem.at[j],
                dot_rsem.at[j],
                {"mp": part},
            )
            for j, part in others()
        ]

    early = min(5, tiles)
    part_width = chunks // 2 * hop_width
    step_width = math.gcd(tile, 256)
    steps = tile // step_width
    lanes = scale_all.shape[1]

    def staged(product, use):
        held = product(0)
        for s in range(1, steps):
            ahead = product(s)
            use(s - 1, held)
            held = ahead
        use(steps - 1, held)

    def fold(values):
        total = values[:, :lanes]
        for c in range(lanes, values.shape[1], lanes):
            total += values[:, c : c + lanes]
        return total

    def spread(values, count):
        return jnp.concatenate([values] * (count // lanes), axis=1)

    def spot(d, i, s):
        return i, slice(d * rows, (d + 1) * rows), slice(s * step_width, (s + 1) * step_width)

    def activate(d, i, kind, rest=None):
        def product(s):
            gate = None
            for cols in rest or [slice(0, full)]:
                piece = w1[i, cols, s * step_width : (s + 1) * step_width]
                term = jnp.dot(u_all[d, :, cols], piece, preferred_element_type=jnp.float32)
                gate = term if gate is None else gate + term
            return gate

        def use(s, gate):
            place = slice(s * step_width, (s + 1) * step_width)
            if rest:
                gate += z_keep[i, :, place].astype(jnp.float32)
            if kind == "other":
                y = (gate * GELU_COEF).astype(jnp.bfloat16)
            else:
                y = (gate * spread(bend_all[...], step_width)).astype(jnp.bfloat16)
                a_keep[i, :, place] = y
            bent, tangent = gelu_tanh(y)
            if kind != "last":
                z_keep[i, :, place] = gelu_value(y, tangent)
            if kind != "own":
                slope = gelu_slope(y, bent, tangent)
                if kind == "last":
                    slope = slope * p_all[spot(d, i, s)]
                    dot_part[...] += fold((slope * y).astype(jnp.float32))
                p_all[spot(d, i, s)] = slope

        staged(product, use)

    def complete(i, kind):
        for s in range(steps):
            place = slice(s * step_width, (s + 1) * step_width)
            y = a_keep[i, :, place].astype(jnp.float32)
            bent, tangent = gelu_tanh(y)
            if kind == "own":
                p_all[spot(0, i, s)] = gelu_slope(y, bent, tangent).astype(jnp.bfloat16)
            else:
                z_keep[i, :, place] = gelu_value(y, tangent).astype(jnp.bfloat16)

    def pregrad(d, i, kind, rest=False):
        begin = part_width if rest else 0

        def product(s):
            piece = w2[i, s * step_width : (s + 1) * step_width, begin:]
            return lax.dot_general(
                e_all[d, :, begin:], piece, CONTRACT_LAST, preferred_element_type=jnp.float32
            )

        def use(s, inner):
            place = slice(s * step_width, (s + 1) * step_width)
            if rest:
                inner += z_keep[i, :, place].astype(jnp.float32)
            if kind != "plain":
                inner = inner * p_all[spot(d, i, s)].astype(jnp.float32)
            if kind == "own":
                dot_part[...] += fold(inner * a_keep[i, :, place].astype(jnp.float32))
            p_all[spot(d, i, s)] = inner.astype(jnp.bfloat16)

        staged(product, use)

    def turn(d, i):
        for s in range(steps):
            place = slice(s * step_width, (s + 1) * step_width)
            down = pl.ds(pl.multiple_of(i * tile + s * step_width, step_width), step_width)
            flipped = z_keep[i, :, place].astype(jnp.float32).T
            zt_all[down, d * rows : (d + 1) * rows] = flipped.astype(jnp.bfloat16)

    def side_start():
        for d in range(1, replicas):
            start(side_copies(d))

    @pl.when(last)
    def _():
        gather_features(cot_ref, e_all.at[0])
        side_start()

        @pl.loop(0, tiles)
        def _(i):
            w_copies(i)[1].wait()
            pregrad(0, i, "plain")

    def mates_sent(ref, which):
        arrived(block_bytes(ref, chips), mate_ssem.at[which])

    def receive(ref, which, begin, end):
        @pl.loop(begin, end)
        def _(q):
            hop_arrived(ref, which, q)
            start(mate_copies(ref, which, q))

    def between(ref, which, work):
        @pl.loop(0, early)
        def _(i):
            work(i)

            @pl.when(i < chunks - chunks // 2)
            def _():
                q = chunks // 2 + i
                hop_arrived(ref, which, q)
                start(mate_copies(ref, which, q))

        receive(ref, which, chunks // 2 + min(early, chunks - chunks // 2), chunks)

    def activate_early(i, cols=slice(0, part_width)):
        w_copies(i)[0].wait()

        def product(s):
            piece = w1[i, cols, s * step_width : (s + 1) * step_width]
            return jnp.dot(u_all[0, :, cols], piece, preferred_element_type=jnp.float32)

        def use(s, gate):
            z_keep[i, :, s * step_width : (s + 1) * step_width] = gate.astype(jnp.bfloat16)

        staged(product, use)

    def pregrad_early(i):
        def product(s):
            piece = w2[i, s * step_width : (s + 1) * step_width, :part_width]
            return lax.dot_general(
                e_all[0, :, :part_width], piece, CONTRACT_LAST, preferred_element_type=jnp.float32
            )

        def use(s, inner):
            z_keep[i, :, s * step_width : (s + 1) * step_width] = inner.astype(jnp.bfloat16)

        staged(product, use)

    def chip_columns(k):
        block = lax.rem(chip + k, chips)
        return pl.ds(pl.multiple_of(block * 2 * width, 2 * width), 2 * width)

    def prepare(cols):
        values = h_all[:, cols].astype(jnp.float32)
        u_all[0, :, cols] = (values * gain_ref[:, cols]).astype(jnp.bfloat16)
        return fold(values * values)

    def close(squares):
        scale = lax.rsqrt(jnp.sum(squares, axis=1, keepdims=True) / full + NORM_EPS)
        scale_all[...] = jnp.broadcast_to(scale, scale_all.shape)
        bend_all[...] = scale_all[...] * GELU_COEF

    @pl.when(first)
    def _():
        def open_tiles(begin, end):
            @pl.loop(begin, end)
            def _(i):
                activate_early(i, chip_columns(0))

        def ready():
            dot_part[...] = prepare(chip_columns(0))
            open_tiles(0, tiles - 1)

        def settle():
            open_tiles(tiles - 1, tiles)
            fetch(1)

        gather_features(x_ref, h_all, (ready, settle))
        squares = dot_part[...]
        for k in range(1, chips):
            squares += prepare(chip_columns(k))
        close(squares)
        dot_part[...] = jnp.zeros_like(dot_part)

    @pl.when(jnp.logical_not(first))
    def _():
        squares = jnp.zeros((rows, lanes), jnp.float32)
        receive(h_all, 0, 0, chunks // 2)
        for q in range(chunks // 2):
            mate_arrived(h_all, 0, q)
            squares += prepare(slice(q * hop_width, (q + 1) * hop_width))
        dot_part[...] = squares
        between(h_all, 0, activate_early)
        squares = dot_part[...]
        for q in range(chunks // 2, chunks):
            mate_arrived(h_all, 0, q)
            squares += prepare(slice(q * hop_width, (q + 1) * hop_width))
        close(squares)
        dot_part[...] = jnp.zeros_like(dot_part)
        mates_sent(h_all, 0)

    def normed():
        values = h_all[...].astype(jnp.float32)
        u_all[0] = (values * scale_all[:, 0:1] * gain_ref[...]).astype(jnp.bfloat16)
        for d in range(1, replicas):
            u_copies(d)[0].start()

    @pl.when(last)
    def _():
        @pl.loop(0, early)
        def _(i):
            activate(0, i, "last", rest=[slice(part_width, full)])

        @pl.loop(early, tiles)
        def _(i):
            w_copies(i)[0].wait()
            activate(0, i, "last")

        start(dot_copies())

    def stream(partial, send, factor, recv, which, pass_block, sending, extra=None):
        @pl.loop(0, blocks)
        def _(b):
            send[:, block_columns(b)] = (partial(b) * factor).astype(jnp.bfloat16)

            @pl.when(sending)
            def _():
                for t in range(span):
                    start(sum_copies(send, recv, which, b * span + t))

            if extra is not None:
                pl.when(b == min(lag, blocks - 1))(extra)

            @pl.when(jnp.logical_and(b >= lag, sending))
            def _():
                pass_block(b - lag)

        @pl.when(sending)
        def _():
            @pl.loop(max(0, blocks - lag), blocks)
            def _(b):
                pass_block(b)

    def pass_on(q):
        total = h_all[my_rows, columns(q)].astype(jnp.float32)
        total += sums[my_rows, columns(q)].astype(jnp.float32)
        sums_arrived(f_recv, 0, q)
        for j in range(parts - 1):
            total += f_recv[j, :, columns(q)].astype(jnp.float32)
        h_hop[:, columns(q)] = total.astype(jnp.bfloat16)
        start(forward_hop(q))

    @pl.when(jnp.logical_not(last))
    def _():
        @pl.when(first)
        def _():
            @pl.loop(0, tiles)
            def _(i):
                activate(0, i, "own", rest=[chip_columns(k) for k in range(1, chips)])

        @pl.when(jnp.logical_not(first))
        def _():
            @pl.loop(0, early)
            def _(i):
                activate(0, i, "own", rest=[slice(part_width, full)])

            @pl.loop(early, tiles)
            def _(i):
                w_copies(i)[0].wait()
                activate(0, i, "own")

        @pl.loop(0, tiles)
        def _(i):
            w_copies(i)[1].wait()

        def partial(b):
            total = jnp.zeros((rows, block_width), jnp.float32)
            for i in range(tiles):
                total += jnp.dot(
                    z_keep[i], w2[i, :, block_columns(b)], preferred_element_type=jnp.float32
                )
            return total

        def pass_block(b):
            for t in range(span):
                pass_on(b * span + t)

        stream(partial, sums, HALF_BACK, f_recv, 0, pass_block, True)

    def replica_forward(kind):
        normed()

        @pl.loop(0, tiles)
        def _(i):
            complete(i, kind)
            turn(0, i)

        for d in range(1, replicas):
            u_copies(d)[0].wait_recv()
            u_copies(d)[1].start()
        flip_u(0)
        for d in range(1, replicas):
            u_copies(d)[1].wait()
            u_copies(d)[0].wait_send()

            @pl.loop(0, tiles)
            def _(i):
                activate(d, i, "other")
                turn(d, i)

            flip_u(d)

    def flip_u(d):
        flipped = u_all[d, :, kept].astype(jnp.float32).T
        ut[:, d * rows : (d + 1) * rows] = flipped.astype(jnp.bfloat16)

    @pl.when(jnp.logical_not(last))
    def _():
        replica_forward("own")
        sent(0)
        receive(e_all.at[0], 1, 0, chunks // 2)
        for q in range(chunks // 2):
            mate_arrived(e_all.at[0], 1, q)
        between(e_all.at[0], 1, pregrad_early)
        for q in range(chunks // 2, chunks):
            mate_arrived(e_all.at[0], 1, q)
        side_start()
        mates_sent(e_all.at[0], 1)

        @pl.loop(0, early)
        def _(i):
            pregrad(0, i, "own", rest=True)

        @pl.loop(early, tiles)
        def _(i):
            pregrad(0, i, "own")

        @pl.when(jnp.logical_not(first))
        def _():
            start(dot_copies())

    def pass_back(q, shift):
        total = sums[my_rows, columns(q)].astype(jnp.float32)
        sums_arrived(b_recv, 1, q)
        for j in range(parts - 1):
            total += b_recv[j, :, columns(q)].astype(jnp.float32)
        scale = scale_all[my_rows, 0:1]
        unit = h_all[my_rows, columns(q)].astype(jnp.float32) * scale
        previous = e_all[0, my_rows, columns(q)].astype(jnp.float32) + scale * (
            total * gain_ref[:, columns(q)] - unit * shift
        )
        g_hop[:, columns(q)] = previous.astype(jnp.bfloat16)
        start(backward_hop(q))

    def row_shift():
        total = dot_part[my_rows, :]
        for j in range(parts - 1):
            total += dot_recv[j]
        return jnp.sum(total, axis=1, keepdims=True) * (HALF_BACK / full)

    def partial(b):
        total = jnp.zeros((rows, block_width), jnp.float32)
        for i in range(tiles):
            total += lax.dot_general(
                p_all[i, 0:rows, :],
                w1[i, block_columns(b), :],
                CONTRACT_LAST,
                preferred_element_type=jnp.float32,
            )
        return total

    def pass_block(b):
        @pl.when(b == 0)
        def _():
            finish(dot_copies())
            dot_recv[0] = jnp.broadcast_to(row_shift(), dot_recv.shape[1:])

        for t in range(span):
            pass_back(b * span + t, dot_recv[0, :, 0:1])

    def extra():
        for d in range(1, replicas):
            arrived(block_bytes(e_all.at[d], chips), side_rsem.at[d])
            start(pass_copies(d))

    stream(partial, sums, 0.5, b_recv, 1, pass_block, jnp.logical_not(first), extra)

    @pl.loop(0, blocks)
    def _(b):
        unit = h_all[:, block_columns(b)].astype(jnp.float32) * spread(scale_all[...], block_width)
        terms = sums[:, block_columns(b)].astype(jnp.float32) * unit
        gain_part[:, block_columns(b)] = jnp.sum(terms.reshape(rows // 8, 8, block_width), axis=0)

    gain_copies = [
        remote(
            gain_part.at[:, pl.ds(pl.multiple_of(part * width, width), width)],
            gain_recv.at[d * parts + j],
            gain_ssem.at[d * parts + j],
            gain_rsem.at[d * parts + j],
            {"dp": other, "mp": part},
        )
        for d, j, other, part in peers
    ]
    start(gain_copies)

    @pl.when(last)
    def _():
        replica_forward("last")

    for d in range(1, replicas):
        arrived(block_bytes(e_all.at[d], chips), pass_rsem.at[d])
        arrived(block_bytes(e_all.at[d], chips), pass_ssem.at[d])
        arrived(block_bytes(e_all.at[d], chips), side_ssem.at[d])
    outs = []
    for d in range(replicas):
        place = pl.ds(d * rows, rows)
        outs.append(
            pltpu.make_async_copy(e_all.at[d, :, kept], e_cols.at[place, :], out_sem.at[d])
        )
    start(outs)
    for d in range(1, replicas):

        @pl.loop(0, tiles)
        def _(i):
            pregrad(d, i, "other")

    total = gain_part[:, my_cols]
    for (d, j, _, _), copy in zip(peers, gain_copies):
        copy.wait()
        total += gain_recv[d * parts + j]
    gain_out[...] = jnp.sum(total, axis=0, keepdims=True)

    finish(outs)

    @pl.when(jnp.logical_not(first))
    def _():
        sent(1)


def weight_grads(
    u_ref, e_ref, gain_ref, p_ref, zt_ref, in_hbm, out_hbm, gain_out, in_buf, out_buf, in_sem, out_sem
):
    tiles, _, tile = in_buf.shape
    gain_out[...] = gain_ref[...]

    def in_copy(i):
        place = pl.ds(pl.multiple_of(i * tile, tile), tile)
        return pltpu.make_async_copy(in_buf.at[i], in_hbm.at[:, place], in_sem.at[i])

    def out_copy(i):
        place = pl.ds(pl.multiple_of(i * tile, tile), tile)
        return pltpu.make_async_copy(out_buf.at[place], out_hbm.at[place], out_sem.at[i])

    @pl.loop(0, tiles)
    def _(i):
        place = pl.ds(pl.multiple_of(i * tile, tile), tile)
        product = jnp.dot(u_ref[...], p_ref[i], preferred_element_type=jnp.float32)
        in_buf[i] = (product * 0.5).astype(in_buf.dtype)
        in_copy(i).start()
        product = jnp.dot(zt_ref[place], e_ref[...], preferred_element_type=jnp.float32)
        out_buf[place] = (product * HALF_BACK).astype(out_buf.dtype)
        out_copy(i).start()

    @pl.loop(0, tiles)
    def _(i):
        in_copy(i).wait()
        out_copy(i).wait()


def shards(inputs, cotangent, gain, weight_in, weight_out):
    stages = lax.axis_size("pipe")
    parts = lax.axis_size("mp")
    replicas = lax.axis_size("dp")
    micro, row_count, width = inputs.shape
    rows = micro * row_count
    full = gain.shape[1]
    hidden = weight_in.shape[2]
    tile = math.gcd(hidden, 1024)
    tiles = hidden // tile
    own = rows // parts
    chips = parts // 2
    half = full // replicas
    hop_width = math.gcd(full, 128)
    chunks = full // hop_width
    span = math.gcd(chunks, 2)
    lanes = 128
    count = replicas * rows
    kept_bytes = 4 * count * (hidden + half) + 65536
    bf16, f32 = jnp.bfloat16, jnp.float32
    vmem = pl.BlockSpec(memory_space=pltpu.VMEM)
    anywhere = pl.BlockSpec(memory_space=pl.ANY)
    dma = pltpu.SemaphoreType.DMA
    zt_all, p_all, u_flip, e_cols, gain_total = pl.pallas_call(
        functools.partial(relay, (stages, parts, replicas, hop_width, span)),
        name="relay",
        out_shape=(
            pltpu.VMEM((hidden, count), bf16),
            pltpu.VMEM((tiles, count, tile), bf16),
            pltpu.VMEM((half, count), bf16),
            pltpu.VMEM((count, half), bf16),
            pltpu.VMEM((1, width), f32),
        ),
        in_specs=[vmem, vmem, vmem, anywhere, anywhere],
        out_specs=(vmem, vmem, vmem, vmem, vmem),
        scratch_shapes=[
            pltpu.VMEM((tiles, full, tile), bf16),
            pltpu.VMEM((tiles, tile, full), bf16),
            pltpu.VMEM((tiles, rows, tile), bf16),
            pltpu.VMEM((tiles, rows, tile), bf16),
            pltpu.VMEM((rows, full), bf16),
            pltpu.VMEM((replicas, rows, full), bf16),
            pltpu.VMEM((replicas, rows, full), bf16),
            pltpu.VMEM((rows, full), bf16),
            pltpu.VMEM((parts - 1, own, full), bf16),
            pltpu.VMEM((parts - 1, own, full), bf16),
            pltpu.VMEM((own, full), bf16),
            pltpu.VMEM((own, full), bf16),
            pltpu.VMEM((rows, lanes), f32),
            pltpu.VMEM((rows, lanes), f32),
            pltpu.VMEM((rows, lanes), f32),
            pltpu.VMEM((parts - 1, own, lanes), f32),
            pltpu.VMEM((8, full), f32),
            pltpu.VMEM((replicas * parts, 8, width), f32),
            dma((tiles,)),
            dma((tiles,)),
            dma((replicas,)),
            dma((parts,)),
            dma((parts,)),
            dma((2,)),
            dma((2, chunks)),
            dma((2,)),
            dma((2, chunks)),
            dma((replicas,)),
            dma((replicas,)),
            dma((replicas,)),
            dma((replicas,)),
            dma((2, replicas)),
            dma((2, replicas)),
            dma((2,)),
            dma((2, chunks)),
            dma((parts,)),
            dma((parts,)),
            dma((replicas * parts,)),
            dma((replicas * parts,)),
        ],
        compiler_params=pltpu.CompilerParams(
            collective_id=0, has_side_effects=True, vmem_limit_bytes=67043328 - kept_bytes
        ),
    )(
        inputs.reshape(rows, width),
        cotangent.reshape(rows, width),
        gain,
        weight_in[0],
        weight_out[0],
    )
    stay = functools.partial(
        pltpu.with_memory_space_constraint, memory_space=pltpu.MemorySpace.VMEM
    )
    grad_first, grad_second, gain_sum = pl.pallas_call(
        weight_grads,
        name="weight_grads",
        out_shape=(
            jax.ShapeDtypeStruct((half, hidden), bf16),
            jax.ShapeDtypeStruct((hidden, half), bf16),
            jax.ShapeDtypeStruct((1, width), f32),
        ),
        in_specs=[vmem, vmem, vmem, vmem, vmem],
        out_specs=(anywhere, anywhere, vmem),
        scratch_shapes=[
            pltpu.VMEM((tiles, half, tile), bf16),
            pltpu.VMEM((hidden, half), bf16),
            dma((tiles,)),
            dma((tiles,)),
        ],
        compiler_params=pltpu.CompilerParams(vmem_limit_bytes=67043328 - kept_bytes),
    )(*(stay(array) for array in (u_flip, e_cols, gain_total, p_all, zt_all)))
    return (grad_first[None], grad_second[None], gain_sum)


def solution(mesh):
    in_specs = (
        P(None, "dp", "mp"),
        P(None, "dp", "mp"),
        P("pipe", None),
        P("pipe", None, "mp"),
        P("pipe", "mp", None),
    )
    out_specs = (P("pipe", "dp", "mp"), P("pipe", "mp", "dp"), P("pipe", "mp"))
    return jax.shard_map(shards, mesh=mesh, in_specs=in_specs, out_specs=out_specs, check_vma=False)
```

```python
import functools
import math

import jax
import jax.numpy as jnp
from jax import lax
from jax.experimental import pallas as pl
from jax.experimental.pallas import tpu as pltpu
from jax.sharding import PartitionSpec as P

GELU_COEF = math.sqrt(2.0 / math.pi)
CUBIC_COEF = 0.044715
NORM_EPS = 1e-06
CONTRACT_LAST = (((1,), (1,)), ((), ()))
MESH = pl.DeviceIdType.MESH


CUBE = CUBIC_COEF / (GELU_COEF * GELU_COEF)
HALF_BACK = 0.5 / GELU_COEF


def gelu_tanh(y):
    bent = y * (CUBE * (y * y))
    return (bent, jnp.tanh(y + bent))


def gelu_value(y, tangent):
    return y * (1.0 + tangent)


def gelu_slope(y, bent, tangent):
    above = 1.0 + tangent
    return above + (1.0 - tangent) * above * (y + 3.0 * bent)


def relay(
    sizes,
    x_ref,
    cot_ref,
    gain_ref,
    w1_hbm,
    w2_hbm,
    zt_all,
    p_all,
    ut,
    e_cols,
    gain_out,
    w1,
    w2,
    z_keep,
    a_keep,
    h_all,
    u_all,
    e_all,
    sums,
    f_recv,
    b_recv,
    h_hop,
    g_hop,
    scale_all,
    bend_all,
    dot_part,
    dot_recv,
    gain_part,
    gain_recv,
    w1_sem,
    w2_sem,
    out_sem,
    x_ssem,
    x_rsem,
    hop_ssem,
    hop_rsem,
    mate_ssem,
    mate_rsem,
    side_ssem,
    side_rsem,
    pass_ssem,
    pass_rsem,
    u_ssem,
    u_rsem,
    rs_ssem,
    rs_rsem,
    dot_ssem,
    dot_rsem,
    gain_ssem,
    gain_rsem,
):
    stages, parts, replicas, hop_width, span = sizes
    sec = lax.axis_index("pipe")
    me = lax.axis_index("mp")
    rep = lax.axis_index("dp")
    tiles, full, tile = w1.shape
    rows = h_all.shape[0]
    own = rows // parts
    width = full // parts
    chunks = full // hop_width
    lag = 2
    first = sec == 0
    last = sec == stages - 1
    chips = parts // 2
    chip, core = me // 2, lax.rem(me, 2)
    mate = chip * 2 + 1 - core

    def w_copies(i):
        start = pl.multiple_of(i * tile, tile)
        return (
            pltpu.make_async_copy(w1_hbm.at[:, pl.ds(start, tile)], w1.at[i], w1_sem.at[i]),
            pltpu.make_async_copy(w2_hbm.at[pl.ds(start, tile), :], w2.at[i], w2_sem.at[i]),
        )

    def fetch(which):
        for i in range(tiles):
            w_copies(i)[which].start()

    fetch(0)

    def across_core(k):
        return lax.rem(chip + k, chips) * 2 + 1 - core

    barrier = pltpu.get_barrier_semaphore()
    peers = []
    for d in range(replicas):
        for j in range(parts):
            if d or j:
                peers.append((d, j, lax.rem(rep + d, replicas), lax.rem(me + j, parts)))
    for _, _, other, part in peers:
        pl.semaphore_signal(
            barrier, inc=1, device_id={"dp": other, "mp": part}, device_id_type=MESH
        )
    for there, absent in ((sec + 1, last), (sec - 1, first)):

        @pl.when(jnp.logical_not(absent))
        def _():
            for k in range(chips):
                pl.semaphore_signal(
                    barrier,
                    inc=1,
                    device_id={"pipe": there, "mp": across_core(k)},
                    device_id_type=MESH,
                )

    neighbours = 2 - first.astype(jnp.int32) - last.astype(jnp.int32)
    dot_part[...] = jnp.zeros_like(dot_part)
    pl.semaphore_wait(barrier, len(peers) + chips * neighbours)

    pl.when(jnp.logical_not(first))(lambda: fetch(1))

    my_rows = pl.ds(pl.multiple_of(me * own, own), own)
    my_cols = pl.ds(pl.multiple_of(me * width, width), width)

    half = full // replicas
    kept = pl.ds(pl.multiple_of(rep * half, half), half)

    def remote(src, dst, ssem, rsem, where):
        return pltpu.make_async_remote_copy(
            src_ref=src,
            dst_ref=dst,
            send_sem=ssem,
            recv_sem=rsem,
            device_id=where,
            device_id_type=MESH,
        )

    def others():
        return [(j, lax.rem(me + j, parts)) for j in range(1, parts)]

    def columns(q):
        return pl.ds(pl.multiple_of(q * hop_width, hop_width), hop_width)

    blocks = chunks // span
    block_width = hop_width * span

    def block_columns(b):
        return pl.ds(pl.multiple_of(b * block_width, block_width), block_width)

    def start(copies):
        for copy in copies:
            copy.start()

    def finish(copies):
        for copy in copies:
            copy.wait()

    def block_rows(k):
        block = lax.rem(chip + chips - k, chips) * 2 + 1 - core
        return pl.ds(pl.multiple_of(block * own, own), own)

    def hop_copies(src, dst, which, q, step):
        return [
            remote(
                src.at[:, columns(q)],
                dst.at[my_rows, columns(q)],
                hop_ssem.at[which],
                hop_rsem.at[which, q],
                {"pipe": lax.rem(sec + step, stages), "mp": across_core(k)},
            )
            for k in range(chips)
        ]

    def forward_hop(q):
        return hop_copies(h_hop, h_all, 0, q, 1)

    def backward_hop(q):
        return hop_copies(g_hop, e_all.at[0], 1, q, stages - 1)

    def arrived(ref, sem):
        pltpu.make_async_copy(ref, ref, sem).wait()

    def block_bytes(ref, count, cols=slice(None)):
        return ref.at[pl.ds(0, count * own), cols]

    def hop_arrived(ref, which, q):
        arrived(block_bytes(ref, chips, columns(q)), hop_rsem.at[which, q])

    def mate_arrived(ref, which, q):
        arrived(block_bytes(ref, chips, columns(q)), mate_rsem.at[which, q])

    def sums_arrived(recv, which, q):
        arrived(recv.at[:, :, columns(q)], rs_rsem.at[which, q])

    def sent(which):
        arrived(block_bytes(h_all, chips), hop_ssem.at[which])
        arrived(block_bytes(h_all, parts - 1), rs_ssem.at[which])

    def mate_copies(ref, which, q):
        copies = []
        for k in range(chips):
            part = ref.at[block_rows(k), columns(q)]
            copies.append(
                remote(part, part, mate_ssem.at[which], mate_rsem.at[which, q], {"mp": mate})
            )
        return copies

    def side_copies(d):
        return [
            remote(
                e_all.at[0, block_rows(k)],
                e_all.at[d, block_rows(k)],
                side_ssem.at[d],
                side_rsem.at[d],
                {"dp": lax.rem(rep + d, replicas)},
            )
            for k in range(chips)
        ]

    def pass_copies(d):
        copies = []
        for k in range(chips):
            part = e_all.at[d, block_rows(k)]
            copies.append(
                remote(part, part, pass_ssem.at[d], pass_rsem.at[d], {"mp": mate})
            )
        return copies

    def u_copies(d):
        part = pl.ds(pl.multiple_of(core * (rows // 2), rows // 2), rows // 2)
        there = {"dp": lax.rem(rep + d, replicas)}
        return (
            remote(u_all.at[0, part], u_all.at[d, part], u_ssem.at[0, d], u_rsem.at[0, d], there),
            remote(
                u_all.at[d, part], u_all.at[d, part], u_ssem.at[1, d], u_rsem.at[1, d], {"mp": mate}
            ),
        )

    def gather_features(src, dst, meanwhile=None):
        def cols(k):
            block = lax.rem(chip + chips - k, chips) * 2 + core
            return pl.ds(pl.multiple_of(block * width, width), width)

        def across(k):
            target = lax.rem(chip + k, chips) * 2 + core
            return remote(src, dst.at[:, my_cols], x_ssem.at[k], x_rsem.at[k], {"mp": target})

        def beside(k):
            part = dst.at[:, cols(k)]
            slot = chips + k
            return remote(
                src if k == 0 else part, part, x_ssem.at[slot], x_rsem.at[slot], {"mp": mate}
            )

        for k in range(1, chips):
            across(k).start()
        beside(0).start()
        dst[:, my_cols] = src[...]
        if meanwhile is not None:
            beside(0).wait_recv()
            meanwhile[0]()
        for k in range(1, chips):
            across(k).wait_recv()
            beside(k).start()
        if meanwhile is not None:
            meanwhile[1]()
        for k in range(1, chips):
            across(k).wait_send()
        beside(0).wait_send()
        if meanwhile is None:
            beside(0).wait_recv()
        for k in range(1, chips):
            beside(k).wait()

    def sum_copies(src, dst, which, q):
        return [
            remote(
                src.at[pl.ds(pl.multiple_of(part * own, own), own), columns(q)],
                dst.at[j - 1, :, columns(q)],
                rs_ssem.at[which],
                rs_rsem.at[which, q],
                {"mp": part},
            )
            for j, part in others()
        ]

    def dot_copies():
        return [
            remote(
                dot_part.at[pl.ds(pl.multiple_of(part * own, own), own)],
                dot_recv.at[j - 1],
                dot_ssem.at[j],
                dot_rsem.at[j],
                {"mp": part},
            )
            for j, part in others()
        ]

    early = min(6, tiles)
    part_width = chunks // 2 * hop_width
    step_width = math.gcd(tile, 256)
    steps = tile // step_width
    lanes = scale_all.shape[1]

    def staged(product, use, group):
        places = [(i, s) for i in group for s in range(steps)]
        held = product(*places[0])
        for before, place in zip(places, places[1:]):
            ahead = product(*place)
            use(*before, held)
            held = ahead
        use(*places[-1], held)

    def grouped(begin, end, work):
        size = 2 if (end - begin) % 2 == 0 else 1

        @pl.loop(0, (end - begin) // size)
        def _(n):
            work([begin + n * size + m for m in range(size)])

    def fold(values):
        total = values[:, :lanes]
        for c in range(lanes, values.shape[1], lanes):
            total += values[:, c : c + lanes]
        return total

    def spread(values, count):
        return jnp.concatenate([values] * (count // lanes), axis=1)

    def spot(d, i, s):
        return i, slice(d * rows, (d + 1) * rows), slice(s * step_width, (s + 1) * step_width)

    def activate(d, group, kind, rest=None):
        def product(i, s):
            gate = None
            for cols in rest or [slice(0, full)]:
                piece = w1[i, cols, s * step_width : (s + 1) * step_width]
                term = jnp.dot(u_all[d, :, cols], piece, preferred_element_type=jnp.float32)
                gate = term if gate is None else gate + term
            return gate

        def use(i, s, gate):
            place = slice(s * step_width, (s + 1) * step_width)
            if rest:
                gate += z_keep[i, :, place].astype(jnp.float32)
            if kind == "other":
                y = (gate * GELU_COEF).astype(jnp.bfloat16)
            else:
                y = (gate * spread(bend_all[...], step_width)).astype(jnp.bfloat16)
                a_keep[i, :, place] = y
            bent, tangent = gelu_tanh(y)
            if kind != "last":
                z_keep[i, :, place] = gelu_value(y, tangent)
            if kind != "own":
                slope = gelu_slope(y, bent, tangent)
                if kind == "last":
                    slope = slope * p_all[spot(d, i, s)]
                    dot_part[...] += fold((slope * y).astype(jnp.float32))
                p_all[spot(d, i, s)] = slope

        staged(product, use, group)

    def complete(i, kind):
        for s in range(steps):
            place = slice(s * step_width, (s + 1) * step_width)
            y = a_keep[i, :, place].astype(jnp.float32)
            bent, tangent = gelu_tanh(y)
            if kind == "own":
                p_all[spot(0, i, s)] = gelu_slope(y, bent, tangent).astype(jnp.bfloat16)
            else:
                z_keep[i, :, place] = gelu_value(y, tangent).astype(jnp.bfloat16)

    def pregrad(d, group, kind, rest=False):
        begin = part_width if rest else 0

        def product(i, s):
            piece = w2[i, s * step_width : (s + 1) * step_width, begin:]
            return lax.dot_general(
                e_all[d, :, begin:], piece, CONTRACT_LAST, preferred_element_type=jnp.float32
            )

        def use(i, s, inner):
            place = slice(s * step_width, (s + 1) * step_width)
            if rest:
                inner += z_keep[i, :, place].astype(jnp.float32)
            if kind != "plain":
                inner = inner * p_all[spot(d, i, s)].astype(jnp.float32)
            if kind == "own":
                dot_part[...] += fold(inner * a_keep[i, :, place].astype(jnp.float32))
            p_all[spot(d, i, s)] = inner.astype(jnp.bfloat16)

        staged(product, use, group)

    def turn(d, i):
        for s in range(steps):
            place = slice(s * step_width, (s + 1) * step_width)
            down = pl.ds(pl.multiple_of(i * tile + s * step_width, step_width), step_width)
            flipped = z_keep[i, :, place].astype(jnp.float32).T
            zt_all[down, d * rows : (d + 1) * rows] = flipped.astype(jnp.bfloat16)

    def side_start():
        for d in range(1, replicas):
            start(side_copies(d))

    @pl.when(last)
    def _():
        gather_features(cot_ref, e_all.at[0])
        side_start()

        def open_inner(group):
            for i in group:
                w_copies(i)[1].wait()
            pregrad(0, group, "plain")

        grouped(0, tiles, open_inner)

    def mates_sent(ref, which):
        arrived(block_bytes(ref, chips), mate_ssem.at[which])

    def receive(ref, which, begin, end):
        @pl.loop(begin, end)
        def _(q):
            hop_arrived(ref, which, q)
            start(mate_copies(ref, which, q))

    def between(ref, which, work):
        @pl.loop(0, early)
        def _(i):
            work(i)

            @pl.when(i < chunks - chunks // 2)
            def _():
                q = chunks // 2 + i
                hop_arrived(ref, which, q)
                start(mate_copies(ref, which, q))

        receive(ref, which, chunks // 2 + min(early, chunks - chunks // 2), chunks)

    def activate_early(i, cols=slice(0, part_width)):
        w_copies(i)[0].wait()

        def product(i, s):
            piece = w1[i, cols, s * step_width : (s + 1) * step_width]
            return jnp.dot(u_all[0, :, cols], piece, preferred_element_type=jnp.float32)

        def use(i, s, gate):
            z_keep[i, :, s * step_width : (s + 1) * step_width] = gate.astype(jnp.bfloat16)

        staged(product, use, [i])

    def pregrad_early(i):
        def product(i, s):
            piece = w2[i, s * step_width : (s + 1) * step_width, :part_width]
            return lax.dot_general(
                e_all[0, :, :part_width], piece, CONTRACT_LAST, preferred_element_type=jnp.float32
            )

        def use(i, s, inner):
            z_keep[i, :, s * step_width : (s + 1) * step_width] = inner.astype(jnp.bfloat16)

        staged(product, use, [i])

    def chip_columns(k):
        block = lax.rem(chip + k, chips)
        return pl.ds(pl.multiple_of(block * 2 * width, 2 * width), 2 * width)

    def prepare(cols):
        values = h_all[:, cols].astype(jnp.float32)
        u_all[0, :, cols] = (values * gain_ref[:, cols]).astype(jnp.bfloat16)
        return fold(values * values)

    def close(squares):
        scale = lax.rsqrt(jnp.sum(squares, axis=1, keepdims=True) / full + NORM_EPS)
        scale_all[...] = jnp.broadcast_to(scale, scale_all.shape)
        bend_all[...] = scale_all[...] * GELU_COEF

    @pl.when(first)
    def _():
        def open_tiles(begin, end):
            @pl.loop(begin, end)
            def _(i):
                activate_early(i, chip_columns(0))

        def ready():
            dot_part[...] = prepare(chip_columns(0))
            open_tiles(0, tiles - 1)

        def settle():
            open_tiles(tiles - 1, tiles)
            fetch(1)

        gather_features(x_ref, h_all, (ready, settle))
        squares = dot_part[...]
        for k in range(1, chips):
            squares += prepare(chip_columns(k))
        close(squares)
        dot_part[...] = jnp.zeros_like(dot_part)

    @pl.when(jnp.logical_not(first))
    def _():
        squares = jnp.zeros((rows, lanes), jnp.float32)
        receive(h_all, 0, 0, chunks // 2)
        for q in range(chunks // 2):
            mate_arrived(h_all, 0, q)
            squares += prepare(slice(q * hop_width, (q + 1) * hop_width))
        dot_part[...] = squares
        between(h_all, 0, activate_early)
        squares = dot_part[...]
        for q in range(chunks // 2, chunks):
            mate_arrived(h_all, 0, q)
            squares += prepare(slice(q * hop_width, (q + 1) * hop_width))
        close(squares)
        dot_part[...] = jnp.zeros_like(dot_part)
        mates_sent(h_all, 0)

    def finish_activation(kind):
        rest = [slice(part_width, full)]
        grouped(0, early, lambda group: activate(0, group, kind, rest=rest))

        def whole(group):
            for i in group:
                w_copies(i)[0].wait()
            activate(0, group, kind)

        grouped(early, tiles, whole)

    def normed():
        values = h_all[...].astype(jnp.float32)
        u_all[0] = (values * scale_all[:, 0:1] * gain_ref[...]).astype(jnp.bfloat16)
        for d in range(1, replicas):
            u_copies(d)[0].start()

    @pl.when(last)
    def _():
        finish_activation("last")

        start(dot_copies())

    def stream(partial, send, factor, recv, which, pass_block, sending, extra=None):
        @pl.loop(0, blocks)
        def _(b):
            send[:, block_columns(b)] = (partial(b) * factor).astype(jnp.bfloat16)

            @pl.when(sending)
            def _():
                for t in range(span):
                    start(sum_copies(send, recv, which, b * span + t))

            if extra is not None:
                pl.when(b == min(lag, blocks - 1))(extra)

            @pl.when(jnp.logical_and(b >= lag, sending))
            def _():
                pass_block(b - lag)

        @pl.when(sending)
        def _():
            @pl.loop(max(0, blocks - lag), blocks)
            def _(b):
                pass_block(b)

    def pass_on(q):
        total = h_all[my_rows, columns(q)].astype(jnp.float32)
        total += sums[my_rows, columns(q)].astype(jnp.float32)
        sums_arrived(f_recv, 0, q)
        for j in range(parts - 1):
            total += f_recv[j, :, columns(q)].astype(jnp.float32)
        h_hop[:, columns(q)] = total.astype(jnp.bfloat16)
        start(forward_hop(q))

    @pl.when(jnp.logical_not(last))
    def _():
        @pl.when(first)
        def _():
            rest = [chip_columns(k) for k in range(1, chips)]
            grouped(0, tiles, lambda group: activate(0, group, "own", rest=rest))

        @pl.when(jnp.logical_not(first))
        def _():
            finish_activation("own")

        @pl.loop(0, tiles)
        def _(i):
            w_copies(i)[1].wait()

        def partial(b):
            total = jnp.zeros((rows, block_width), jnp.float32)
            for i in range(tiles):
                total += jnp.dot(
                    z_keep[i], w2[i, :, block_columns(b)], preferred_element_type=jnp.float32
                )
            return total

        def pass_block(b):
            for t in range(span):
                pass_on(b * span + t)

        stream(partial, sums, HALF_BACK, f_recv, 0, pass_block, True)

    def replica_forward(kind):
        normed()

        @pl.loop(0, tiles)
        def _(i):
            complete(i, kind)
            turn(0, i)

        for d in range(1, replicas):
            u_copies(d)[0].wait_recv()
            u_copies(d)[1].start()
        flip_u(0)
        for d in range(1, replicas):
            u_copies(d)[1].wait()
            u_copies(d)[0].wait_send()

            def other(group):
                activate(d, group, "other")
                for i in group:
                    turn(d, i)

            grouped(0, tiles, other)

            flip_u(d)

    def flip_u(d):
        flipped = u_all[d, :, kept].astype(jnp.float32).T
        ut[:, d * rows : (d + 1) * rows] = flipped.astype(jnp.bfloat16)

    @pl.when(jnp.logical_not(last))
    def _():
        replica_forward("own")
        sent(0)
        receive(e_all.at[0], 1, 0, chunks // 2)
        for q in range(chunks // 2):
            mate_arrived(e_all.at[0], 1, q)
        between(e_all.at[0], 1, pregrad_early)
        for q in range(chunks // 2, chunks):
            mate_arrived(e_all.at[0], 1, q)
        side_start()
        mates_sent(e_all.at[0], 1)

        grouped(0, early, lambda group: pregrad(0, group, "own", rest=True))
        grouped(early, tiles, lambda group: pregrad(0, group, "own"))

        @pl.when(jnp.logical_not(first))
        def _():
            start(dot_copies())

    def pass_back(q, shift):
        total = sums[my_rows, columns(q)].astype(jnp.float32)
        sums_arrived(b_recv, 1, q)
        for j in range(parts - 1):
            total += b_recv[j, :, columns(q)].astype(jnp.float32)
        scale = scale_all[my_rows, 0:1]
        unit = h_all[my_rows, columns(q)].astype(jnp.float32) * scale
        previous = e_all[0, my_rows, columns(q)].astype(jnp.float32) + scale * (
            total * gain_ref[:, columns(q)] - unit * shift
        )
        g_hop[:, columns(q)] = previous.astype(jnp.bfloat16)
        start(backward_hop(q))

    def row_shift():
        total = dot_part[my_rows, :]
        for j in range(parts - 1):
            total += dot_recv[j]
        return jnp.sum(total, axis=1, keepdims=True) * (HALF_BACK / full)

    def partial(b):
        total = jnp.zeros((rows, block_width), jnp.float32)
        for i in range(tiles):
            total += lax.dot_general(
                p_all[i, 0:rows, :],
                w1[i, block_columns(b), :],
                CONTRACT_LAST,
                preferred_element_type=jnp.float32,
            )
        return total

    def pass_block(b):
        @pl.when(b == 0)
        def _():
            finish(dot_copies())
            dot_recv[0] = jnp.broadcast_to(row_shift(), dot_recv.shape[1:])

        for t in range(span):
            pass_back(b * span + t, dot_recv[0, :, 0:1])

    def extra():
        for d in range(1, replicas):
            arrived(block_bytes(e_all.at[d], chips), side_rsem.at[d])
            start(pass_copies(d))

    stream(partial, sums, 0.5, b_recv, 1, pass_block, jnp.logical_not(first), extra)

    @pl.loop(0, blocks)
    def _(b):
        unit = h_all[:, block_columns(b)].astype(jnp.float32) * spread(scale_all[...], block_width)
        terms = sums[:, block_columns(b)].astype(jnp.float32) * unit
        gain_part[:, block_columns(b)] = jnp.sum(terms.reshape(rows // 8, 8, block_width), axis=0)

    gain_copies = [
        remote(
            gain_part.at[:, pl.ds(pl.multiple_of(part * width, width), width)],
            gain_recv.at[d * parts + j],
            gain_ssem.at[d * parts + j],
            gain_rsem.at[d * parts + j],
            {"dp": other, "mp": part},
        )
        for d, j, other, part in peers
    ]
    start(gain_copies)

    @pl.when(last)
    def _():
        replica_forward("last")

    for d in range(1, replicas):
        arrived(block_bytes(e_all.at[d], chips), pass_rsem.at[d])
        arrived(block_bytes(e_all.at[d], chips), pass_ssem.at[d])
        arrived(block_bytes(e_all.at[d], chips), side_ssem.at[d])
    outs = []
    for d in range(replicas):
        place = pl.ds(d * rows, rows)
        outs.append(
            pltpu.make_async_copy(e_all.at[d, :, kept], e_cols.at[place, :], out_sem.at[d])
        )
    start(outs)
    for d in range(1, replicas):

        grouped(0, tiles, lambda group: pregrad(d, group, "other"))

    total = gain_part[:, my_cols]
    for (d, j, _, _), copy in zip(peers, gain_copies):
        copy.wait()
        total += gain_recv[d * parts + j]
    gain_out[...] = jnp.sum(total, axis=0, keepdims=True)

    finish(outs)

    @pl.when(jnp.logical_not(first))
    def _():
        sent(1)


def weight_grads(
    u_ref, e_ref, gain_ref, p_ref, zt_ref, in_hbm, out_hbm, gain_out, in_buf, out_buf, in_sem, out_sem
):
    tiles, _, tile = in_buf.shape
    gain_out[...] = gain_ref[...]

    def in_copy(i):
        place = pl.ds(i * tile, tile)
        return pltpu.make_async_copy(in_buf.at[i], in_hbm.at[:, place], in_sem.at[i])

    def out_copy(i):
        place = pl.ds(i * tile, tile)
        return pltpu.make_async_copy(out_buf.at[place], out_hbm.at[place], out_sem.at[i])

    for i in range(tiles):
        place = slice(i * tile, (i + 1) * tile)
        product = jnp.dot(u_ref[...], p_ref[i], preferred_element_type=jnp.float32)
        in_buf[i] = (product * 0.5).astype(in_buf.dtype)
        in_copy(i).start()
        product = jnp.dot(zt_ref[place], e_ref[...], preferred_element_type=jnp.float32)
        out_buf[place] = (product * HALF_BACK).astype(out_buf.dtype)
        out_copy(i).start()

    for i in range(tiles):
        in_copy(i).wait()
        out_copy(i).wait()


def shards(inputs, cotangent, gain, weight_in, weight_out):
    stages = lax.axis_size("pipe")
    parts = lax.axis_size("mp")
    replicas = lax.axis_size("dp")
    micro, row_count, width = inputs.shape
    rows = micro * row_count
    full = gain.shape[1]
    hidden = weight_in.shape[2]
    tile = math.gcd(hidden, 1024)
    tiles = hidden // tile
    own = rows // parts
    chips = parts // 2
    half = full // replicas
    hop_width = math.gcd(full, 128)
    chunks = full // hop_width
    span = math.gcd(chunks, 2)
    lanes = 128
    count = replicas * rows
    kept_bytes = 4 * count * (hidden + half) + 16384
    bf16, f32 = jnp.bfloat16, jnp.float32
    vmem = pl.BlockSpec(memory_space=pltpu.VMEM)
    anywhere = pl.BlockSpec(memory_space=pl.ANY)
    dma = pltpu.SemaphoreType.DMA
    zt_all, p_all, u_flip, e_cols, gain_total = pl.pallas_call(
        functools.partial(relay, (stages, parts, replicas, hop_width, span)),
        name="relay",
        out_shape=(
            pltpu.VMEM((hidden, count), bf16),
            pltpu.VMEM((tiles, count, tile), bf16),
            pltpu.VMEM((half, count), bf16),
            pltpu.VMEM((count, half), bf16),
            pltpu.VMEM((1, width), f32),
        ),
        in_specs=[vmem, vmem, vmem, anywhere, anywhere],
        out_specs=(vmem, vmem, vmem, vmem, vmem),
        scratch_shapes=[
            pltpu.VMEM((tiles, full, tile), bf16),
            pltpu.VMEM((tiles, tile, full), bf16),
            pltpu.VMEM((tiles, rows, tile), bf16),
            pltpu.VMEM((tiles, rows, tile), bf16),
            pltpu.VMEM((rows, full), bf16),
            pltpu.VMEM((replicas, rows, full), bf16),
            pltpu.VMEM((replicas, rows, full), bf16),
            pltpu.VMEM((rows, full), bf16),
            pltpu.VMEM((parts - 1, own, full), bf16),
            pltpu.VMEM((parts - 1, own, full), bf16),
            pltpu.VMEM((own, full), bf16),
            pltpu.VMEM((own, full), bf16),
            pltpu.VMEM((rows, lanes), f32),
            pltpu.VMEM((rows, lanes), f32),
            pltpu.VMEM((rows, lanes), f32),
            pltpu.VMEM((parts - 1, own, lanes), f32),
            pltpu.VMEM((8, full), f32),
            pltpu.VMEM((replicas * parts, 8, width), f32),
            dma((tiles,)),
            dma((tiles,)),
            dma((replicas,)),
            dma((parts,)),
            dma((parts,)),
            dma((2,)),
            dma((2, chunks)),
            dma((2,)),
            dma((2, chunks)),
            dma((replicas,)),
            dma((replicas,)),
            dma((replicas,)),
            dma((replicas,)),
            dma((2, replicas)),
            dma((2, replicas)),
            dma((2,)),
            dma((2, chunks)),
            dma((parts,)),
            dma((parts,)),
            dma((replicas * parts,)),
            dma((replicas * parts,)),
        ],
        compiler_params=pltpu.CompilerParams(
            collective_id=0, has_side_effects=True, vmem_limit_bytes=67043328 - kept_bytes
        ),
    )(
        inputs.reshape(rows, width),
        cotangent.reshape(rows, width),
        gain,
        weight_in[0],
        weight_out[0],
    )
    stay = functools.partial(
        pltpu.with_memory_space_constraint, memory_space=pltpu.MemorySpace.VMEM
    )
    grad_first, grad_second, gain_sum = pl.pallas_call(
        weight_grads,
        name="weight_grads",
        out_shape=(
            jax.ShapeDtypeStruct((half, hidden), bf16),
            jax.ShapeDtypeStruct((hidden, half), bf16),
            jax.ShapeDtypeStruct((1, width), f32),
        ),
        in_specs=[vmem, vmem, vmem, vmem, vmem],
        out_specs=(anywhere, anywhere, vmem),
        scratch_shapes=[
            pltpu.VMEM((tiles, half, tile), bf16),
            pltpu.VMEM((hidden, half), bf16),
            dma((tiles,)),
            dma((tiles,)),
        ],
        compiler_params=pltpu.CompilerParams(vmem_limit_bytes=67043328 - kept_bytes),
    )(*(stay(array) for array in (u_flip, e_cols, gain_total, p_all, zt_all)))
    return (grad_first[None], grad_second[None], gain_sum)


def solution(mesh):
    in_specs = (
        P(None, "dp", "mp"),
        P(None, "dp", "mp"),
        P("pipe", None),
        P("pipe", None, "mp"),
        P("pipe", "mp", None),
    )
    out_specs = (P("pipe", "dp", "mp"), P("pipe", "mp", "dp"), P("pipe", "mp"))
    return jax.shard_map(shards, mesh=mesh, in_specs=in_specs, out_specs=out_specs, check_vma=False)
```

```python
import functools
import math

import jax
import jax.numpy as jnp
from jax import lax
from jax.experimental import pallas as pl
from jax.experimental.pallas import tpu as pltpu
from jax.sharding import PartitionSpec as P

GELU_COEF = math.sqrt(2.0 / math.pi)
CUBIC_COEF = 0.044715
NORM_EPS = 1e-06
CONTRACT_LAST = (((1,), (1,)), ((), ()))
MESH = pl.DeviceIdType.MESH


CUBE = CUBIC_COEF / (GELU_COEF * GELU_COEF)
HALF_BACK = 0.5 / GELU_COEF


def gelu_tanh(y):
    bent = y * (CUBE * (y * y))
    return (bent, jnp.tanh(y + bent))


def gelu_value(y, tangent):
    return y * (1.0 + tangent)


def gelu_slope(y, bent, tangent):
    above = 1.0 + tangent
    return above + (1.0 - tangent) * above * (y + 3.0 * bent)


def relay(
    sizes,
    x_ref,
    cot_ref,
    gain_ref,
    w1_hbm,
    w2_hbm,
    zt_all,
    p_all,
    ut,
    e_cols,
    gain_out,
    w1,
    w2,
    z_keep,
    a_keep,
    h_all,
    u_all,
    e_all,
    sums,
    f_recv,
    b_recv,
    h_hop,
    g_hop,
    scale_all,
    bend_all,
    dot_part,
    dot_recv,
    gain_part,
    gain_recv,
    w1_sem,
    w2_sem,
    out_sem,
    x_ssem,
    x_rsem,
    hop_ssem,
    hop_rsem,
    mate_ssem,
    mate_rsem,
    side_ssem,
    side_rsem,
    pass_ssem,
    pass_rsem,
    u_ssem,
    u_rsem,
    rs_ssem,
    rs_rsem,
    dot_ssem,
    dot_rsem,
    gain_ssem,
    gain_rsem,
):
    stages, parts, replicas, hop_width, span = sizes
    sec = lax.axis_index("pipe")
    me = lax.axis_index("mp")
    rep = lax.axis_index("dp")
    tiles, full, tile = w1.shape
    rows = h_all.shape[0]
    own = rows // parts
    width = full // parts
    chunks = full // hop_width
    lag = 2
    first = sec == 0
    last = sec == stages - 1
    chips = parts // 2
    chip, core = me // 2, lax.rem(me, 2)
    mate = chip * 2 + 1 - core

    def w_copies(i):
        start = pl.multiple_of(i * tile, tile)
        return (
            pltpu.make_async_copy(w1_hbm.at[:, pl.ds(start, tile)], w1.at[i], w1_sem.at[i]),
            pltpu.make_async_copy(w2_hbm.at[pl.ds(start, tile), :], w2.at[i], w2_sem.at[i]),
        )

    def fetch(which):
        for i in range(tiles):
            w_copies(i)[which].start()

    fetch(0)

    def across_core(k):
        return lax.rem(chip + k, chips) * 2 + 1 - core

    barrier = pltpu.get_barrier_semaphore()
    peers = []
    for d in range(replicas):
        for j in range(parts):
            if d or j:
                peers.append((d, j, lax.rem(rep + d, replicas), lax.rem(me + j, parts)))
    for _, _, other, part in peers:
        pl.semaphore_signal(
            barrier, inc=1, device_id={"dp": other, "mp": part}, device_id_type=MESH
        )
    for there, absent in ((sec + 1, last), (sec - 1, first)):

        @pl.when(jnp.logical_not(absent))
        def _():
            for k in range(chips):
                pl.semaphore_signal(
                    barrier,
                    inc=1,
                    device_id={"pipe": there, "mp": across_core(k)},
                    device_id_type=MESH,
                )

    neighbours = 2 - first.astype(jnp.int32) - last.astype(jnp.int32)
    dot_part[...] = jnp.zeros_like(dot_part)
    pl.semaphore_wait(barrier, len(peers) + chips * neighbours)

    pl.when(jnp.logical_not(first))(lambda: fetch(1))

    my_rows = pl.ds(pl.multiple_of(me * own, own), own)
    my_cols = pl.ds(pl.multiple_of(me * width, width), width)

    half = full // replicas
    kept = pl.ds(pl.multiple_of(rep * half, half), half)

    def remote(src, dst, ssem, rsem, where):
        return pltpu.make_async_remote_copy(
            src_ref=src,
            dst_ref=dst,
            send_sem=ssem,
            recv_sem=rsem,
            device_id=where,
            device_id_type=MESH,
        )

    def others():
        return [(j, lax.rem(me + j, parts)) for j in range(1, parts)]

    def columns(q):
        return pl.ds(pl.multiple_of(q * hop_width, hop_width), hop_width)

    blocks = chunks // span
    block_width = hop_width * span

    def block_columns(b):
        return pl.ds(pl.multiple_of(b * block_width, block_width), block_width)

    def start(copies):
        for copy in copies:
            copy.start()

    def finish(copies):
        for copy in copies:
            copy.wait()

    def block_rows(k):
        block = lax.rem(chip + chips - k, chips) * 2 + 1 - core
        return pl.ds(pl.multiple_of(block * own, own), own)

    def hop_copies(src, dst, which, q, step):
        return [
            remote(
                src.at[:, columns(q)],
                dst.at[my_rows, columns(q)],
                hop_ssem.at[which],
                hop_rsem.at[which, q],
                {"pipe": lax.rem(sec + step, stages), "mp": across_core(k)},
            )
            for k in range(chips)
        ]

    def forward_hop(q):
        return hop_copies(h_hop, h_all, 0, q, 1)

    def backward_hop(q):
        return hop_copies(g_hop, e_all.at[0], 1, q, stages - 1)

    def arrived(ref, sem):
        pltpu.make_async_copy(ref, ref, sem).wait()

    def block_bytes(ref, count, cols=slice(None)):
        return ref.at[pl.ds(0, count * own), cols]

    def hop_arrived(ref, which, q):
        arrived(block_bytes(ref, chips, columns(q)), hop_rsem.at[which, q])

    def mate_arrived(ref, which, q):
        arrived(block_bytes(ref, chips, columns(q)), mate_rsem.at[which, q])

    def sums_arrived(recv, which, q):
        arrived(recv.at[:, :, columns(q)], rs_rsem.at[which, q])

    def sent(which):
        arrived(block_bytes(h_all, chips), hop_ssem.at[which])
        arrived(block_bytes(h_all, parts - 1), rs_ssem.at[which])

    def mate_copies(ref, which, q):
        copies = []
        for k in range(chips):
            part = ref.at[block_rows(k), columns(q)]
            copies.append(
                remote(part, part, mate_ssem.at[which], mate_rsem.at[which, q], {"mp": mate})
            )
        return copies

    def side_copies(d):
        return [
            remote(
                e_all.at[0, block_rows(k)],
                e_all.at[d, block_rows(k)],
                side_ssem.at[d],
                side_rsem.at[d],
                {"dp": lax.rem(rep + d, replicas)},
            )
            for k in range(chips)
        ]

    def pass_copies(d):
        copies = []
        for k in range(chips):
            part = e_all.at[d, block_rows(k)]
            copies.append(
                remote(part, part, pass_ssem.at[d], pass_rsem.at[d], {"mp": mate})
            )
        return copies

    def u_copies(d):
        part = pl.ds(pl.multiple_of(core * (rows // 2), rows // 2), rows // 2)
        there = {"dp": lax.rem(rep + d, replicas)}
        return (
            remote(u_all.at[0, part], u_all.at[d, part], u_ssem.at[0, d], u_rsem.at[0, d], there),
            remote(
                u_all.at[d, part], u_all.at[d, part], u_ssem.at[1, d], u_rsem.at[1, d], {"mp": mate}
            ),
        )

    def gather_features(src, dst, meanwhile=None):
        def cols(k):
            block = lax.rem(chip + chips - k, chips) * 2 + core
            return pl.ds(pl.multiple_of(block * width, width), width)

        def across(k):
            target = lax.rem(chip + k, chips) * 2 + core
            return remote(src, dst.at[:, my_cols], x_ssem.at[k], x_rsem.at[k], {"mp": target})

        def beside(k):
            part = dst.at[:, cols(k)]
            slot = chips + k
            return remote(
                src if k == 0 else part, part, x_ssem.at[slot], x_rsem.at[slot], {"mp": mate}
            )

        for k in range(1, chips):
            across(k).start()
        beside(0).start()
        dst[:, my_cols] = src[...]
        if meanwhile is not None:
            beside(0).wait_recv()
            meanwhile[0]()
        for k in range(1, chips):
            across(k).wait_recv()
            beside(k).start()
        if meanwhile is not None:
            meanwhile[1]()
        for k in range(1, chips):
            across(k).wait_send()
        beside(0).wait_send()
        if meanwhile is None:
            beside(0).wait_recv()
        for k in range(1, chips):
            beside(k).wait()

    def sum_copies(src, dst, which, q):
        return [
            remote(
                src.at[pl.ds(pl.multiple_of(part * own, own), own), columns(q)],
                dst.at[j - 1, :, columns(q)],
                rs_ssem.at[which],
                rs_rsem.at[which, q],
                {"mp": part},
            )
            for j, part in others()
        ]

    def dot_copies():
        return [
            remote(
                dot_part.at[pl.ds(pl.multiple_of(part * own, own), own)],
                dot_recv.at[j - 1],
                dot_ssem.at[j],
                dot_rsem.at[j],
                {"mp": part},
            )
            for j, part in others()
        ]

    early = min(6, tiles)
    part_width = chunks // 2 * hop_width
    step_width = math.gcd(tile, 256)
    steps = tile // step_width
    lanes = scale_all.shape[1]

    def staged(product, use, group):
        places = [(i, s) for i in group for s in range(steps)]
        held = product(*places[0])
        for before, place in zip(places, places[1:]):
            ahead = product(*place)
            use(*before, held)
            held = ahead
        use(*places[-1], held)

    def grouped(begin, end, work, most=2):
        size = max(n for n in range(1, most + 1) if (end - begin) % n == 0)

        @pl.loop(0, (end - begin) // size)
        def _(n):
            work([begin + n * size + m for m in range(size)])

    def fold(values):
        total = values[:, :lanes]
        for c in range(lanes, values.shape[1], lanes):
            total += values[:, c : c + lanes]
        return total

    def spread(values, count):
        return jnp.concatenate([values] * (count // lanes), axis=1)

    def spot(d, i, s):
        return i, slice(d * rows, (d + 1) * rows), slice(s * step_width, (s + 1) * step_width)

    def activate(d, group, kind, rest=None):
        def product(i, s):
            gate = None
            for cols in rest or [slice(0, full)]:
                piece = w1[i, cols, s * step_width : (s + 1) * step_width]
                term = jnp.dot(u_all[d, :, cols], piece, preferred_element_type=jnp.float32)
                gate = term if gate is None else gate + term
            return gate

        def use(i, s, gate):
            place = slice(s * step_width, (s + 1) * step_width)
            if rest:
                gate += z_keep[i, :, place].astype(jnp.float32)
            if kind == "other":
                y = (gate * GELU_COEF).astype(jnp.bfloat16)
            else:
                y = (gate * spread(bend_all[...], step_width)).astype(jnp.bfloat16)
                a_keep[i, :, place] = y
            bent, tangent = gelu_tanh(y)
            if kind != "last":
                z_keep[i, :, place] = gelu_value(y, tangent)
            if kind != "own":
                slope = gelu_slope(y, bent, tangent)
                if kind == "last":
                    slope = slope * p_all[spot(d, i, s)]
                    dot_part[...] += fold((slope * y).astype(jnp.float32))
                p_all[spot(d, i, s)] = slope

        staged(product, use, group)

    def complete(i, kind):
        for s in range(steps):
            place = slice(s * step_width, (s + 1) * step_width)
            y = a_keep[i, :, place].astype(jnp.float32)
            bent, tangent = gelu_tanh(y)
            if kind == "own":
                p_all[spot(0, i, s)] = gelu_slope(y, bent, tangent).astype(jnp.bfloat16)
            else:
                z_keep[i, :, place] = gelu_value(y, tangent).astype(jnp.bfloat16)

    def pregrad(d, group, kind, rest=False):
        begin = part_width if rest else 0

        def product(i, s):
            piece = w2[i, s * step_width : (s + 1) * step_width, begin:]
            return lax.dot_general(
                e_all[d, :, begin:], piece, CONTRACT_LAST, preferred_element_type=jnp.float32
            )

        def use(i, s, inner):
            place = slice(s * step_width, (s + 1) * step_width)
            if rest:
                inner += z_keep[i, :, place].astype(jnp.float32)
            if kind != "plain":
                inner = inner * p_all[spot(d, i, s)].astype(jnp.float32)
            if kind == "own":
                dot_part[...] += fold(inner * a_keep[i, :, place].astype(jnp.float32))
            p_all[spot(d, i, s)] = inner.astype(jnp.bfloat16)

        staged(product, use, group)

    def turn(d, i):
        for s in range(steps):
            place = slice(s * step_width, (s + 1) * step_width)
            down = pl.ds(pl.multiple_of(i * tile + s * step_width, step_width), step_width)
            flipped = z_keep[i, :, place].astype(jnp.float32).T
            zt_all[down, d * rows : (d + 1) * rows] = flipped.astype(jnp.bfloat16)

    def side_start():
        for d in range(1, replicas):
            start(side_copies(d))

    @pl.when(last)
    def _():
        gather_features(cot_ref, e_all.at[0])
        side_start()

        def open_inner(group):
            for i in group:
                w_copies(i)[1].wait()
            pregrad(0, group, "plain")

        grouped(0, tiles, open_inner)

    def mates_sent(ref, which):
        arrived(block_bytes(ref, chips), mate_ssem.at[which])

    def receive(ref, which, begin, end):
        @pl.loop(begin, end)
        def _(q):
            hop_arrived(ref, which, q)
            start(mate_copies(ref, which, q))

    def between(ref, which, work):
        @pl.loop(0, early)
        def _(i):
            work(i)

            @pl.when(i < chunks - chunks // 2)
            def _():
                q = chunks // 2 + i
                hop_arrived(ref, which, q)
                start(mate_copies(ref, which, q))

        receive(ref, which, chunks // 2 + min(early, chunks - chunks // 2), chunks)

    def activate_early(i, cols=slice(0, part_width)):
        w_copies(i)[0].wait()

        def product(i, s):
            piece = w1[i, cols, s * step_width : (s + 1) * step_width]
            return jnp.dot(u_all[0, :, cols], piece, preferred_element_type=jnp.float32)

        def use(i, s, gate):
            z_keep[i, :, s * step_width : (s + 1) * step_width] = gate.astype(jnp.bfloat16)

        staged(product, use, [i])

    def pregrad_early(i):
        def product(i, s):
            piece = w2[i, s * step_width : (s + 1) * step_width, :part_width]
            return lax.dot_general(
                e_all[0, :, :part_width], piece, CONTRACT_LAST, preferred_element_type=jnp.float32
            )

        def use(i, s, inner):
            z_keep[i, :, s * step_width : (s + 1) * step_width] = inner.astype(jnp.bfloat16)

        staged(product, use, [i])

    def chip_columns(k):
        block = lax.rem(chip + k, chips)
        return pl.ds(pl.multiple_of(block * 2 * width, 2 * width), 2 * width)

    def prepare(cols):
        values = h_all[:, cols].astype(jnp.float32)
        u_all[0, :, cols] = (values * gain_ref[:, cols]).astype(jnp.bfloat16)
        return fold(values * values)

    def close(squares):
        scale = lax.rsqrt(jnp.sum(squares, axis=1, keepdims=True) / full + NORM_EPS)
        scale_all[...] = jnp.broadcast_to(scale, scale_all.shape)
        bend_all[...] = scale_all[...] * GELU_COEF

    @pl.when(first)
    def _():
        def open_tiles(begin, end):
            @pl.loop(begin, end)
            def _(i):
                activate_early(i, chip_columns(0))

        def ready():
            dot_part[...] = prepare(chip_columns(0))
            open_tiles(0, tiles - 1)

        def settle():
            open_tiles(tiles - 1, tiles)
            fetch(1)

        gather_features(x_ref, h_all, (ready, settle))
        squares = dot_part[...]
        for k in range(1, chips):
            squares += prepare(chip_columns(k))
        close(squares)
        dot_part[...] = jnp.zeros_like(dot_part)

    @pl.when(jnp.logical_not(first))
    def _():
        squares = jnp.zeros((rows, lanes), jnp.float32)
        receive(h_all, 0, 0, chunks // 2)
        for q in range(chunks // 2):
            mate_arrived(h_all, 0, q)
            squares += prepare(slice(q * hop_width, (q + 1) * hop_width))
        dot_part[...] = squares
        between(h_all, 0, activate_early)
        squares = dot_part[...]
        for q in range(chunks // 2, chunks):
            mate_arrived(h_all, 0, q)
            squares += prepare(slice(q * hop_width, (q + 1) * hop_width))
        close(squares)
        dot_part[...] = jnp.zeros_like(dot_part)
        mates_sent(h_all, 0)

    def finish_activation(kind):
        rest = [slice(part_width, full)]
        grouped(0, early, lambda group: activate(0, group, kind, rest=rest), 3)

        def whole(group):
            for i in group:
                w_copies(i)[0].wait()
            activate(0, group, kind)

        grouped(early, tiles, whole)

    def normed():
        values = h_all[...].astype(jnp.float32)
        u_all[0] = (values * scale_all[:, 0:1] * gain_ref[...]).astype(jnp.bfloat16)
        for d in range(1, replicas):
            u_copies(d)[0].start()

    @pl.when(last)
    def _():
        finish_activation("last")

        start(dot_copies())

    def stream(partial, send, factor, recv, which, pass_block, sending, extra=None):
        @pl.loop(0, blocks)
        def _(b):
            send[:, block_columns(b)] = (partial(b) * factor).astype(jnp.bfloat16)

            @pl.when(sending)
            def _():
                for t in range(span):
                    start(sum_copies(send, recv, which, b * span + t))

            if extra is not None:
                pl.when(b == min(lag, blocks - 1))(extra)

            @pl.when(jnp.logical_and(b >= lag, sending))
            def _():
                pass_block(b - lag)

        @pl.when(sending)
        def _():
            @pl.loop(max(0, blocks - lag), blocks)
            def _(b):
                pass_block(b)

    def pass_on(q):
        total = h_all[my_rows, columns(q)].astype(jnp.float32)
        total += sums[my_rows, columns(q)].astype(jnp.float32)
        sums_arrived(f_recv, 0, q)
        for j in range(parts - 1):
            total += f_recv[j, :, columns(q)].astype(jnp.float32)
        h_hop[:, columns(q)] = total.astype(jnp.bfloat16)
        start(forward_hop(q))

    @pl.when(jnp.logical_not(last))
    def _():
        @pl.when(first)
        def _():
            rest = [chip_columns(k) for k in range(1, chips)]
            grouped(0, tiles, lambda group: activate(0, group, "own", rest=rest))

        @pl.when(jnp.logical_not(first))
        def _():
            finish_activation("own")

        @pl.loop(0, tiles)
        def _(i):
            w_copies(i)[1].wait()

        def partial(b):
            total = jnp.zeros((rows, block_width), jnp.float32)
            for i in range(tiles):
                total += jnp.dot(
                    z_keep[i], w2[i, :, block_columns(b)], preferred_element_type=jnp.float32
                )
            return total

        def pass_block(b):
            for t in range(span):
                pass_on(b * span + t)

        stream(partial, sums, HALF_BACK, f_recv, 0, pass_block, True)

    def replica_forward(kind):
        normed()

        @pl.loop(0, tiles)
        def _(i):
            complete(i, kind)
            turn(0, i)

        for d in range(1, replicas):
            u_copies(d)[0].wait_recv()
            u_copies(d)[1].start()
        flip_u(0)
        for d in range(1, replicas):
            u_copies(d)[1].wait()
            u_copies(d)[0].wait_send()

            def other(group):
                activate(d, group, "other")
                for i in group:
                    turn(d, i)

            grouped(0, tiles, other)

            flip_u(d)

    def flip_u(d):
        flipped = u_all[d, :, kept].astype(jnp.float32).T
        ut[:, d * rows : (d + 1) * rows] = flipped.astype(jnp.bfloat16)

    @pl.when(jnp.logical_not(last))
    def _():
        replica_forward("own")
        sent(0)
        receive(e_all.at[0], 1, 0, chunks // 2)
        for q in range(chunks // 2):
            mate_arrived(e_all.at[0], 1, q)
        between(e_all.at[0], 1, pregrad_early)
        for q in range(chunks // 2, chunks):
            mate_arrived(e_all.at[0], 1, q)
        side_start()
        mates_sent(e_all.at[0], 1)

        grouped(0, early, lambda group: pregrad(0, group, "own", rest=True), 3)
        grouped(early, tiles, lambda group: pregrad(0, group, "own"))

        @pl.when(jnp.logical_not(first))
        def _():
            start(dot_copies())

    def pass_back(q, shift):
        total = sums[my_rows, columns(q)].astype(jnp.float32)
        sums_arrived(b_recv, 1, q)
        for j in range(parts - 1):
            total += b_recv[j, :, columns(q)].astype(jnp.float32)
        scale = scale_all[my_rows, 0:1]
        unit = h_all[my_rows, columns(q)].astype(jnp.float32) * scale
        previous = e_all[0, my_rows, columns(q)].astype(jnp.float32) + scale * (
            total * gain_ref[:, columns(q)] - unit * shift
        )
        g_hop[:, columns(q)] = previous.astype(jnp.bfloat16)
        start(backward_hop(q))

    def row_shift():
        total = dot_part[my_rows, :]
        for j in range(parts - 1):
            total += dot_recv[j]
        return jnp.sum(total, axis=1, keepdims=True) * (HALF_BACK / full)

    def partial(b):
        total = jnp.zeros((rows, block_width), jnp.float32)
        for i in range(tiles):
            total += lax.dot_general(
                p_all[i, 0:rows, :],
                w1[i, block_columns(b), :],
                CONTRACT_LAST,
                preferred_element_type=jnp.float32,
            )
        return total

    def pass_block(b):
        @pl.when(b == 0)
        def _():
            finish(dot_copies())
            dot_recv[0] = jnp.broadcast_to(row_shift(), dot_recv.shape[1:])

        for t in range(span):
            pass_back(b * span + t, dot_recv[0, :, 0:1])

    def extra():
        for d in range(1, replicas):
            arrived(block_bytes(e_all.at[d], chips), side_rsem.at[d])
            start(pass_copies(d))

    def gain_block(b, values):
        unit = h_all[:, block_columns(b)].astype(jnp.float32) * spread(scale_all[...], block_width)
        terms = (values * unit).reshape(rows // 8, 8, block_width)
        gain_part[:, block_columns(b)] = jnp.sum(terms, axis=0)

    @pl.when(jnp.logical_not(first))
    def _():
        stream(partial, sums, 0.5, b_recv, 1, pass_block, True, extra)

        @pl.loop(0, blocks)
        def _(b):
            gain_block(b, sums[:, block_columns(b)].astype(jnp.float32))

    @pl.when(first)
    def _():
        @pl.loop(0, blocks)
        def _(b):
            gain_block(b, partial(b) * 0.5)
            pl.when(b == min(lag, blocks - 1))(extra)

    gain_copies = [
        remote(
            gain_part.at[:, pl.ds(pl.multiple_of(part * width, width), width)],
            gain_recv.at[d * parts + j],
            gain_ssem.at[d * parts + j],
            gain_rsem.at[d * parts + j],
            {"dp": other, "mp": part},
        )
        for d, j, other, part in peers
    ]
    start(gain_copies)

    @pl.when(last)
    def _():
        replica_forward("last")

    for d in range(1, replicas):
        arrived(block_bytes(e_all.at[d], chips), pass_rsem.at[d])
        arrived(block_bytes(e_all.at[d], chips), pass_ssem.at[d])
        arrived(block_bytes(e_all.at[d], chips), side_ssem.at[d])
    outs = []
    for d in range(replicas):
        place = pl.ds(d * rows, rows)
        outs.append(
            pltpu.make_async_copy(e_all.at[d, :, kept], e_cols.at[place, :], out_sem.at[d])
        )
    start(outs)
    for d in range(1, replicas):

        grouped(0, tiles, lambda group: pregrad(d, group, "other"), 4)

    total = gain_part[:, my_cols]
    for (d, j, _, _), copy in zip(peers, gain_copies):
        copy.wait()
        total += gain_recv[d * parts + j]
    gain_out[...] = jnp.sum(total, axis=0, keepdims=True)

    finish(outs)

    @pl.when(jnp.logical_not(first))
    def _():
        sent(1)


def weight_grads(
    u_ref, e_ref, gain_ref, p_ref, zt_ref, in_hbm, out_hbm, gain_out, in_buf, out_buf, in_sem, out_sem
):
    tiles, _, tile = in_buf.shape
    gain_out[...] = gain_ref[...]

    def in_copy(i):
        place = pl.ds(i * tile, tile)
        return pltpu.make_async_copy(in_buf.at[i], in_hbm.at[:, place], in_sem.at[i])

    def out_copy(i):
        place = pl.ds(i * tile, tile)
        return pltpu.make_async_copy(out_buf.at[place], out_hbm.at[place], out_sem.at[i])

    for i in range(tiles):
        place = slice(i * tile, (i + 1) * tile)
        product = jnp.dot(u_ref[...], p_ref[i], preferred_element_type=jnp.float32)
        in_buf[i] = (product * 0.5).astype(in_buf.dtype)
        in_copy(i).start()
        product = jnp.dot(zt_ref[place], e_ref[...], preferred_element_type=jnp.float32)
        out_buf[place] = (product * HALF_BACK).astype(out_buf.dtype)
        out_copy(i).start()

    for i in range(tiles):
        in_copy(i).wait()
        out_copy(i).wait()


def shards(inputs, cotangent, gain, weight_in, weight_out):
    stages = lax.axis_size("pipe")
    parts = lax.axis_size("mp")
    replicas = lax.axis_size("dp")
    micro, row_count, width = inputs.shape
    rows = micro * row_count
    full = gain.shape[1]
    hidden = weight_in.shape[2]
    tile = math.gcd(hidden, 1024)
    tiles = hidden // tile
    own = rows // parts
    chips = parts // 2
    half = full // replicas
    hop_width = math.gcd(full, 128)
    chunks = full // hop_width
    span = math.gcd(chunks, 2)
    lanes = 128
    count = replicas * rows
    kept_bytes = 4 * count * (hidden + half) + 16384
    bf16, f32 = jnp.bfloat16, jnp.float32
    vmem = pl.BlockSpec(memory_space=pltpu.VMEM)
    anywhere = pl.BlockSpec(memory_space=pl.ANY)
    dma = pltpu.SemaphoreType.DMA
    zt_all, p_all, u_flip, e_cols, gain_total = pl.pallas_call(
        functools.partial(relay, (stages, parts, replicas, hop_width, span)),
        name="relay",
        out_shape=(
            pltpu.VMEM((hidden, count), bf16),
            pltpu.VMEM((tiles, count, tile), bf16),
            pltpu.VMEM((half, count), bf16),
            pltpu.VMEM((count, half), bf16),
            pltpu.VMEM((1, width), f32),
        ),
        in_specs=[vmem, vmem, vmem, anywhere, anywhere],
        out_specs=(vmem, vmem, vmem, vmem, vmem),
        scratch_shapes=[
            pltpu.VMEM((tiles, full, tile), bf16),
            pltpu.VMEM((tiles, tile, full), bf16),
            pltpu.VMEM((tiles, rows, tile), bf16),
            pltpu.VMEM((tiles, rows, tile), bf16),
            pltpu.VMEM((rows, full), bf16),
            pltpu.VMEM((replicas, rows, full), bf16),
            pltpu.VMEM((replicas, rows, full), bf16),
            pltpu.VMEM((rows, full), bf16),
            pltpu.VMEM((parts - 1, own, full), bf16),
            pltpu.VMEM((parts - 1, own, full), bf16),
            pltpu.VMEM((own, full), bf16),
            pltpu.VMEM((own, full), bf16),
            pltpu.VMEM((rows, lanes), f32),
            pltpu.VMEM((rows, lanes), f32),
            pltpu.VMEM((rows, lanes), f32),
            pltpu.VMEM((parts - 1, own, lanes), f32),
            pltpu.VMEM((8, full), f32),
            pltpu.VMEM((replicas * parts, 8, width), f32),
            dma((tiles,)),
            dma((tiles,)),
            dma((replicas,)),
            dma((parts,)),
            dma((parts,)),
            dma((2,)),
            dma((2, chunks)),
            dma((2,)),
            dma((2, chunks)),
            dma((replicas,)),
            dma((replicas,)),
            dma((replicas,)),
            dma((replicas,)),
            dma((2, replicas)),
            dma((2, replicas)),
            dma((2,)),
            dma((2, chunks)),
            dma((parts,)),
            dma((parts,)),
            dma((replicas * parts,)),
            dma((replicas * parts,)),
        ],
        compiler_params=pltpu.CompilerParams(
            collective_id=0, has_side_effects=True, vmem_limit_bytes=67043328 - kept_bytes
        ),
    )(
        inputs.reshape(rows, width),
        cotangent.reshape(rows, width),
        gain,
        weight_in[0],
        weight_out[0],
    )
    stay = functools.partial(
        pltpu.with_memory_space_constraint, memory_space=pltpu.MemorySpace.VMEM
    )
    grad_first, grad_second, gain_sum = pl.pallas_call(
        weight_grads,
        name="weight_grads",
        out_shape=(
            jax.ShapeDtypeStruct((half, hidden), bf16),
            jax.ShapeDtypeStruct((hidden, half), bf16),
            jax.ShapeDtypeStruct((1, width), f32),
        ),
        in_specs=[vmem, vmem, vmem, vmem, vmem],
        out_specs=(anywhere, anywhere, vmem),
        scratch_shapes=[
            pltpu.VMEM((tiles, half, tile), bf16),
            pltpu.VMEM((hidden, half), bf16),
            dma((tiles,)),
            dma((tiles,)),
        ],
        compiler_params=pltpu.CompilerParams(vmem_limit_bytes=67043328 - kept_bytes),
    )(*(stay(array) for array in (u_flip, e_cols, gain_total, p_all, zt_all)))
    return (grad_first[None], grad_second[None], gain_sum)


def solution(mesh):
    in_specs = (
        P(None, "dp", "mp"),
        P(None, "dp", "mp"),
        P("pipe", None),
        P("pipe", None, "mp"),
        P("pipe", "mp", None),
    )
    out_specs = (P("pipe", "dp", "mp"), P("pipe", "mp", "dp"), P("pipe", "mp"))
    return jax.shard_map(shards, mesh=mesh, in_specs=in_specs, out_specs=out_specs, check_vma=False)
```
